32 devices in a mesh: gx: 4 (over y, x), gy: 8 (over z, core).
Axes of the slice: x: 2, y: 2, z: 4, core: 2. Of those that a mesh axis runs over, the one named last changes fastest.
Arguments:
- electric: float32 [3, 128, 6144], P(None, 'gx', 'gy'), may hold values from -6 to 6
- magnetic: float32 [3, 128, 6144], P(None, 'gx', 'gy'), may hold values from -6 to 6
- tensor: float32 [9, 128, 6144], P(None, 'gx', 'gy'), may hold values from -0.15 to 1
- saved: bfloat16 [6, 3, 128, 6144], P(None, None, 'gx', 'gy'), may hold values from -6 to 6
Outputs:
- adj_electric: float32 [3, 128, 6144], P(None, 'gx', 'gy')
- adj_magnetic: float32 [3, 128, 6144], P(None, 'gx', 'gy')
- gradient: float32 [128, 6144], P('gx', 'gy')
The draws below stay inside these ranges and needn't reach their ends.
All inputs are finite; a program needn't handle non-finite values.
Results may differ from the reference program's by a relative error of at most 0.0003.
Values sent between devices are 32-bit elements; how exact they have to be, the bound alone decides.
No kernel may reach another device: no remote copies, remote signals or barrier semaphores. Data moves between devices by JAX's collectives and lax.ppermute only.
A program may use at most 64 MiB of HBM per device.

```python
import math
import jax
import jax.numpy as jnp
from jax import lax

NZ = 48
STEPS = 6
RADIUS = 8
NX = 128
NY = 128


def draw_tensor(key, part):
    first, second = jax.random.split(jax.random.fold_in(key, 7))
    shape = (9, NX, NY * NZ)
    diagonal = jnp.exp(jax.random.uniform(first, shape, jnp.float32, math.log(0.25), 0.0))
    others = jax.random.uniform(second, shape, jnp.float32, -0.15, 0.15)
    on_diagonal = (jnp.arange(9) % 4 == 0)[:, None, None]
    return jnp.where(on_diagonal, diagonal, others)


def level_of(own_key, shape, cuts, smallest, largest):
    def one(axis_at, shards_of):
        draws = jax.random.uniform(jax.random.fold_in(jax.random.fold_in(own_key, 6), axis_at), (shards_of,), jnp.float32, smallest / len(cuts), largest / len(cuts))
        return jnp.repeat(jnp.exp(draws), shape[axis_at] // shards_of).reshape((-1,) + (1,) * (len(shape) - axis_at - 1))

    factor_of = one(*cuts[0])
    for cut in cuts[1:]:
        factor_of = factor_of * one(*cut)
    return factor_of


def bell_draw(rng, extent, scale, reach, cuts=(), kind=jnp.bfloat16):
    array = jax.random.normal(rng, extent, jnp.float32) * scale
    if len(cuts) > 0:
        array = level_of(rng, extent, cuts, -0.22, 0.18) * array
    return jnp.clip(array, min=-reach, max=reach).astype(kind)


def setup_inputs(seed: int = 0) -> dict:
    key_list = jax.random.split(jax.random.key(seed), 5)
    electric = bell_draw(key_list[0], (3, NX, NY * NZ), 1.0, 6.0, ((1, 4), (2, 8)), jnp.float32)
    magnetic = bell_draw(key_list[1], (3, NX, NY * NZ), 1.0, 6.0, ((1, 4), (2, 8)), jnp.float32)
    tensor = draw_tensor(jax.random.fold_in(key_list[4], 71), 0)
    saved = bell_draw(key_list[3], (STEPS, 3, NX, NY * NZ), 1.0, 6.0, ((2, 4), (3, 8)))
    return {"electric": electric, "magnetic": magnetic, "tensor": tensor, "saved": saved}


courant = 0.45


def ahead(field, axis):
    moved = jnp.concatenate([lax.slice_in_dim(field, 1, field.shape[axis], axis=axis), jnp.zeros_like(lax.slice_in_dim(field, 0, 1, axis=axis))], axis=axis)
    return moved - field


def behind(field, axis):
    moved = jnp.concatenate([jnp.zeros_like(lax.slice_in_dim(field, 0, 1, axis=axis)), lax.slice_in_dim(field, 0, field.shape[axis] - 1, axis=axis)], axis=axis)
    return field - moved


def tent(offset):
    return (RADIUS + 1.0 - abs(offset)) / (RADIUS + 1.0)


def coverage(length):
    places = jnp.arange(length, dtype=jnp.int32)
    total = jnp.zeros((length,), jnp.float32)
    for offset in range(-RADIUS, RADIUS + 1):
        inside = ((places + offset >= 0) & (places + offset < length)).astype(jnp.float32)
        total = total + tent(offset) * inside
    return total


def reference(electric, magnetic, tensor, saved):
    shape = (NX, NY, NZ)
    fields_e = [electric[index].reshape(shape) for index in range(3)]
    fields_h = [magnetic[index].reshape(shape) for index in range(3)]
    mats = [tensor[index].reshape(shape) for index in range(9)]
    corr = jnp.zeros(shape, jnp.float32)
    for section in range(STEPS):
        scaled_e = [(mats[col] * fields_e[0] + mats[3 + col] * fields_e[1]) + mats[6 + col] * fields_e[2] for col in range(3)]
        curl_zero = ahead(scaled_e[2], 1) - ahead(scaled_e[1], 2)
        curl_one = ahead(scaled_e[0], 2) - ahead(scaled_e[2], 0)
        curl_two = ahead(scaled_e[1], 0) - ahead(scaled_e[0], 1)
        fields_h = [fields_h[0] - courant * curl_zero, fields_h[1] - courant * curl_one, fields_h[2] - courant * curl_two]
        back_zero = behind(fields_h[2], 1) - behind(fields_h[1], 2)
        back_one = behind(fields_h[0], 2) - behind(fields_h[2], 0)
        back_two = behind(fields_h[1], 0) - behind(fields_h[0], 1)
        fields_e = [fields_e[0] + courant * back_zero, fields_e[1] + courant * back_one, fields_e[2] + courant * back_two]
        frame = saved[section].astype(jnp.float32)
        corr = corr + ((fields_e[0] * frame[0].reshape(shape) + fields_e[1] * frame[1].reshape(shape)) + fields_e[2] * frame[2].reshape(shape))
    adj_electric = jnp.stack([item.reshape(NX, NY * NZ) for item in fields_e])
    adj_magnetic = jnp.stack([item.reshape(NX, NY * NZ) for item in fields_h])
    cover = coverage(NX)[:, None] * jnp.repeat(coverage(NY), NZ)[None, :]
    scaled = corr.reshape(NX, NY * NZ) / cover
    padded = jnp.pad(scaled, ((RADIUS, RADIUS), (0, 0)))
    across = tent(-RADIUS) * padded[0:NX]
    for offset in range(-RADIUS + 1, RADIUS + 1):
        across = across + tent(offset) * padded[RADIUS + offset:RADIUS + offset + NX]
    padded = jnp.pad(across, ((0, 0), (RADIUS * NZ, RADIUS * NZ)))
    span = NY * NZ
    gradient = tent(-RADIUS) * padded[:, 0:span]
    for offset in range(-RADIUS + 1, RADIUS + 1):
        start = (RADIUS + offset) * NZ
        gradient = gradient + tent(offset) * padded[:, start:start + span]
    return adj_electric, adj_magnetic, gradient
```

```python
import jax
import jax.numpy as jnp
from jax import lax
from jax.sharding import PartitionSpec as P

NZ = 48
STEPS = 6
RADIUS = 8


courant = 0.45


def swap_pairs(count, first):
    pairs = []
    for i in range(first, count - 1, 2):
        pairs += [(i, i + 1), (i + 1, i)]
    return pairs


def swap(first, last, axis):
    count = lax.axis_size(axis)
    even = lax.axis_index(axis) % 2 == 0
    from_a = lax.ppermute(jnp.where(even, last, first), axis, swap_pairs(count, 0))
    from_b = lax.ppermute(jnp.where(even, first, last), axis, swap_pairs(count, 1))
    return jnp.where(even, from_b, from_a), jnp.where(even, from_a, from_b)


def tent(offset):
    return (RADIUS + 1.0 - abs(offset)) / (RADIUS + 1.0)


def coverage(places, length):
    total = jnp.zeros(places.shape, jnp.float32)
    for offset in range(-RADIUS, RADIUS + 1):
        inside = ((places + offset >= 0) & (places + offset < length)).astype(jnp.float32)
        total = total + tent(offset) * inside
    return total


def filter_rows(extended, tile_rows):
    result = tent(-RADIUS) * extended[0:tile_rows]
    for offset in range(-RADIUS + 1, RADIUS + 1):
        result = result + tent(offset) * extended[RADIUS + offset : RADIUS + offset + tile_rows]
    return result


def filter_columns(extended, tile_width):
    result = tent(-RADIUS) * extended[:, 0:tile_width]
    for offset in range(-RADIUS + 1, RADIUS + 1):
        begin = (RADIUS + offset) * NZ
        result = result + tent(offset) * extended[:, begin : begin + tile_width]
    return result


def leapfrog(fields_e, fields_h, mats, upper_mask, lower_mask, inside):
    rows, width = fields_e[0].shape
    zero_row = jnp.zeros((1, width), jnp.float32)
    zero_y = jnp.zeros((rows, NZ), jnp.float32)
    zero_z = jnp.zeros((rows, 1), jnp.float32)

    def next_x(field):
        return jnp.concatenate([field[1:], zero_row], axis=0) - field

    def next_y(field):
        return jnp.concatenate([field[:, NZ:], zero_y], axis=1) - field

    def next_z(field):
        return jnp.concatenate([field[:, 1:], zero_z], axis=1) * upper_mask - field

    def prev_x(field):
        return field - jnp.concatenate([zero_row, field[:-1]], axis=0)

    def prev_y(field):
        return field - jnp.concatenate([zero_y, field[:, :-NZ]], axis=1)

    def prev_z(field):
        return field - jnp.concatenate([zero_z, field[:, :-1]], axis=1) * lower_mask

    g = [
        mats[col] * fields_e[0] + mats[3 + col] * fields_e[1] + mats[6 + col] * fields_e[2]
        for col in range(3)
    ]
    fields_h = [
        (fields_h[0] - courant * (next_y(g[2]) - next_z(g[1]))) * inside,
        (fields_h[1] - courant * (next_z(g[0]) - next_x(g[2]))) * inside,
        (fields_h[2] - courant * (next_x(g[1]) - next_y(g[0]))) * inside,
    ]
    h = fields_h
    fields_e = [
        fields_e[0] + courant * (prev_y(h[2]) - prev_z(h[1])),
        fields_e[1] + courant * (prev_z(h[0]) - prev_x(h[2])),
        fields_e[2] + courant * (prev_x(h[1]) - prev_y(h[0])),
    ]
    return fields_e, fields_h


def shards(electric, magnetic, tensor, saved):
    tile_rows, tile_width = electric.shape[1:]
    tile_cols = tile_width // NZ
    halo = STEPS
    side = halo * NZ
    parts = [*electric, *magnetic, *tensor]
    n = len(parts)

    def stack_rows(begin):
        return jnp.concatenate([p[begin : begin + halo] for p in parts], axis=0)

    def stack_lanes(begin):
        return jnp.concatenate([p[:, begin : begin + side] for p in parts], axis=1)

    low_x, high_x = swap(stack_rows(0), stack_rows(tile_rows - halo), "gx")
    low_y, high_y = swap(stack_lanes(0), stack_lanes(tile_width - side), "gy")
    both_x = [low_x, high_x]

    def corners(begin):
        return jnp.concatenate([b[:, begin : begin + side] for b in both_x], axis=1)

    low_c, high_c = swap(corners(0), corners(tile_width - side), "gy")

    def extend(k):
        rows = slice(k * halo, (k + 1) * halo)
        lanes = slice(k * side, (k + 1) * side)
        mid = jnp.concatenate([low_x[rows], parts[k], high_x[rows]], axis=0)
        low = jnp.concatenate([low_c[rows, :side], low_y[:, lanes], low_c[rows, side:]], axis=0)
        high = jnp.concatenate([high_c[rows, :side], high_y[:, lanes], high_c[rows, side:]], axis=0)
        return jnp.concatenate([low, mid, high], axis=1)

    ext = [extend(k) for k in range(n)]
    fields_e, fields_h, mats = ext[0:3], ext[3:6], ext[6:15]
    shape = ext[0].shape
    lane = lax.broadcasted_iota(jnp.int32, shape, 1)
    row = lax.broadcasted_iota(jnp.int32, shape, 0)
    depth = lane % NZ
    upper_mask = (depth != NZ - 1).astype(jnp.float32)
    lower_mask = (depth != 0).astype(jnp.float32)
    inside = (
        (row + lax.axis_index("gx") * tile_rows >= halo)
        & (lane + lax.axis_index("gy") * tile_width >= side)
    ).astype(jnp.float32)

    def own(x):
        return x[halo : halo + tile_rows, side : side + tile_width]

    corr = jnp.zeros((tile_rows, tile_width), jnp.float32)
    for section in range(STEPS):
        fields_e, fields_h = leapfrog(fields_e, fields_h, mats, upper_mask, lower_mask, inside)
        frame = saved[section].astype(jnp.float32)
        corr = corr + (own(fields_e[0]) * frame[0] + own(fields_e[1]) * frame[1] + own(fields_e[2]) * frame[2])

    row_places = lax.axis_index("gx") * tile_rows + jnp.arange(tile_rows, dtype=jnp.int32)
    col_places = lax.axis_index("gy") * tile_cols + jnp.arange(tile_cols, dtype=jnp.int32)
    cover_rows = coverage(row_places, lax.axis_size("gx") * tile_rows)
    cover_cols = jnp.repeat(coverage(col_places, lax.axis_size("gy") * tile_cols), NZ)
    cover = cover_rows[:, None] * cover_cols[None, :]
    scaled = corr / cover
    low, high = swap(scaled[:RADIUS], scaled[-RADIUS:], "gx")
    across = filter_rows(jnp.concatenate([low, scaled, high], axis=0), tile_rows)
    reach = RADIUS * NZ
    low, high = swap(across[:, :reach], across[:, -reach:], "gy")
    gradient = filter_columns(jnp.concatenate([low, across, high], axis=1), tile_width)
    return (jnp.stack([own(x) for x in fields_e]), jnp.stack([own(x) for x in fields_h]), gradient)


def solution(mesh):
    in_specs = (
        P(None, "gx", "gy"),
        P(None, "gx", "gy"),
        P(None, "gx", "gy"),
        P(None, None, "gx", "gy"),
    )
    out_specs = (P(None, "gx", "gy"), P(None, "gx", "gy"), P("gx", "gy"))
    return jax.shard_map(shards, mesh=mesh, in_specs=in_specs, out_specs=out_specs, check_vma=False)
```

```python
import functools

import jax
import jax.numpy as jnp
from jax import lax
from jax.experimental import pallas as pl
from jax.experimental.pallas import tpu as pltpu
from jax.sharding import PartitionSpec as P

NZ = 48
STEPS = 6
RADIUS = 8
SUB = 8
LANE = 128

courant = 0.45


def up_to(size, unit):
    return -(-size // unit) * unit


HALO = STEPS
SIDE = up_to(HALO * NZ, LANE)
REACH = RADIUS * NZ


def swap_pairs(count, first):
    pairs = []
    for i in range(first, count - 1, 2):
        pairs += [(i, i + 1), (i + 1, i)]
    return pairs


def swap(to_a, to_b, axis):
    count = lax.axis_size(axis)
    from_b = lax.ppermute(to_b, axis, swap_pairs(count, 1))
    from_a = lax.ppermute(to_a, axis, swap_pairs(count, 0))
    return from_a, from_b


def is_even(axis):
    return lax.rem(lax.axis_index(axis), 2) == 0


def call(body, outs, ins, scratch=(), limit=16):
    vmem = pl.BlockSpec(memory_space=pltpu.VMEM)
    return pl.pallas_call(
        body,
        out_shape=[jax.ShapeDtypeStruct(s, jnp.float32) for s in outs],
        in_specs=[vmem] * len(ins),
        out_specs=[vmem] * len(outs),
        scratch_shapes=list(scratch),
        compiler_params=pltpu.CompilerParams(vmem_limit_bytes=limit * 2**20),
    )(*ins)


def pack_rows(first_e, last_e, first_h, last_h, first_t, last_t, to_a, to_b):
    even = is_even("gx")
    at = 0
    for first, last in ((first_e, last_e), (first_h, last_h), (first_t, last_t)):
        for c in range(first.shape[0]):
            head = first[c, 0:HALO, :]
            tail = last[c, SUB - HALO : SUB, :]
            to_a[at : at + HALO, :] = jnp.where(even, tail, head)
            to_b[at : at + HALO, :] = jnp.where(even, head, tail)
            at += HALO


def pack_x(electric, magnetic, tensor):
    rows, width = electric.shape[1:]
    parts = (electric, magnetic, tensor)
    ins, specs = [], []
    for part in parts:
        for block in (0, rows // SUB - 1):
            ins.append(part)
            specs.append(pl.BlockSpec((part.shape[0], SUB, width), lambda i, block=block: (0, block, 0)))
    packed = HALO * sum(part.shape[0] for part in parts)
    out = jax.ShapeDtypeStruct((packed, width), jnp.float32)
    return pl.pallas_call(
        pack_rows,
        grid=(1,),
        out_shape=[out, out],
        in_specs=specs,
        out_specs=[pl.BlockSpec((packed, width), lambda i: (0, 0))] * 2,
        compiler_params=pltpu.CompilerParams(vmem_limit_bytes=8 * 2**20),
    )(*ins)


def pack_lanes(size, *refs):
    ins, (to_a, to_b) = refs[:-2], refs[-2:]
    even = is_even("gy")
    at = 0
    for ref in ins:
        width = ref.shape[2]
        for c in range(ref.shape[0]):
            head = ref[c, :, 0:size]
            tail = ref[c, :, width - size : width]
            to_a[at] = jnp.where(even, tail, head)
            to_b[at] = jnp.where(even, head, tail)
            at += 1


def pack_y(size, *ins):
    out = (sum(x.shape[0] for x in ins), ins[0].shape[1], size)
    return call(functools.partial(pack_lanes, size), [out, out], ins)


def main_body(
    e_in, h_in, t_in, saved, xa, xb, ya, yb, ca, cb, inverse, e_out, h_out, scaled, to_a, to_b, fe, fh, ft
):
    rows, width = e_in.shape[1:]
    total_rows, total = fe.shape[1:]
    tiles = total_rows // SUB
    even_x, even_y = is_even("gx"), is_even("gy")
    inner = slice(SUB, SUB + rows)
    middle = slice(SIDE, SIDE + width)
    left, right = slice(0, SIDE), slice(SIDE + width, total)
    top, bottom = slice(0, SUB), slice(SUB + rows, total_rows)
    top_in = slice(SUB - HALO, SUB)
    bottom_in = slice(SUB + rows, SUB + rows + HALO)

    k = 0
    for own, full, factor in ((e_in, fe, None), (h_in, fh, courant), (t_in, ft, courant * courant)):
        for c in range(own.shape[0]):

            def put(where_rows, where_lanes, value, full=full, c=c, factor=factor):
                full[c, where_rows, where_lanes] = value if factor is None else value * factor

            packed = slice(k * HALO, (k + 1) * HALO)
            full[c, top, :] = jnp.zeros((SUB, total), jnp.float32)
            full[c, bottom, :] = jnp.zeros((SUB, total), jnp.float32)
            put(inner, middle, own[c])
            a, b = ya[k], yb[k]
            put(inner, left, jnp.where(even_y, b, a))
            put(inner, right, jnp.where(even_y, a, b))
            a, b = xa[packed], xb[packed]
            put(top_in, middle, jnp.where(even_x, b, a))
            put(bottom_in, middle, jnp.where(even_x, a, b))
            aa, ab, ba, bb = ca[0, packed], cb[0, packed], ca[1, packed], cb[1, packed]
            left_a, left_b = jnp.where(even_y, ab, aa), jnp.where(even_y, bb, ba)
            put(top_in, left, jnp.where(even_x, left_b, left_a))
            put(bottom_in, left, jnp.where(even_x, left_a, left_b))
            right_a, right_b = jnp.where(even_y, aa, ab), jnp.where(even_y, ba, bb)
            put(top_in, right, jnp.where(even_x, right_b, right_a))
            put(bottom_in, right, jnp.where(even_x, right_a, right_b))
            k += 1

    inside_x = jnp.where(lax.axis_index("gx") > 0, 1.0, 0.0).astype(jnp.float32)
    inside_y = jnp.where(lax.axis_index("gy") > 0, 1.0, 0.0).astype(jnp.float32)

    for step in range(STEPS):
        left_over = STEPS - step
        begin = (SIDE - left_over * NZ) // LANE * LANE
        end = up_to(SIDE + width + left_over * NZ, LANE)
        span = end - begin
        lanes = slice(begin, end)
        sub = lax.broadcasted_iota(jnp.int32, (SUB, span), 0)
        depth = lax.rem(lax.broadcasted_iota(jnp.int32, (SUB, span), 1) + (begin % NZ), NZ)
        upper = (depth != NZ - 1).astype(jnp.float32)
        lower = (depth != 0).astype(jnp.float32)
        low = SIDE - begin
        last = step == STEPS - 1

        def tile(ref, c, r):
            return ref[c, r * SUB : (r + 1) * SUB, lanes]

        def to_tile(ref, c, r, value):
            ref[c, r * SUB : (r + 1) * SUB, lanes] = value

        def from_next_y(f):
            return pltpu.roll(f, span - NZ, 1)

        def from_next_z(f):
            return pltpu.roll(f, span - 1, 1) * upper

        def from_prev_y(f):
            return pltpu.roll(f, NZ, 1)

        def from_prev_z(f):
            return pltpu.roll(f, 1, 1) * lower

        after = None
        for r in reversed(range(tiles)):
            e = [tile(fe, c, r) for c in range(3)]
            g = [
                (tile(ft, c, r) * e[0] + tile(ft, 3 + c, r) * e[1]) + tile(ft, 6 + c, r) * e[2]
                for c in range(3)
            ]
            turned = [None] + [pltpu.roll(g[c], SUB - 1, 0) for c in (1, 2)]
            if after is None:
                after = turned
            if not (last and r == tiles - 1):
                next_x = [None] + [jnp.where(sub == SUB - 1, after[c], turned[c]) for c in (1, 2)]
                curl = [
                    (from_next_y(g[2]) - g[2]) - (from_next_z(g[1]) - g[1]),
                    (from_next_z(g[0]) - g[0]) - (next_x[2] - g[2]),
                    (next_x[1] - g[1]) - (from_next_y(g[0]) - g[0]),
                ]
                for c in range(3):
                    h = tile(fh, c, r) - curl[c]
                    if r == 0:
                        h = h * inside_x
                    h = jnp.concatenate([h[:, :low] * inside_y, h[:, low:]], axis=1)
                    to_tile(fh, c, r, h)
            after = turned

        before = None
        for r in range(tiles):
            if last and r == tiles - 1:
                continue
            h = [tile(fh, c, r) for c in range(3)]
            turned = [None] + [pltpu.roll(h[c], 1, 0) for c in (1, 2)]
            if before is None:
                before = turned
            if not (last and r == 0):
                prev_x = [None] + [jnp.where(sub == 0, before[c], turned[c]) for c in (1, 2)]
                curl = [
                    (h[2] - from_prev_y(h[2])) - (h[1] - from_prev_z(h[1])),
                    (h[0] - from_prev_z(h[0])) - (h[2] - prev_x[2]),
                    (h[1] - prev_x[1]) - (h[0] - from_prev_y(h[0])),
                ]
                for c in range(3):
                    to_tile(fe, c, r, tile(fe, c, r) + curl[c])
            before = turned

        pair = 2 * SUB
        for r in range(rows // pair):
            at = slice(r * pair, (r + 1) * pair)
            at_full = slice(SUB + r * pair, SUB + (r + 1) * pair)
            s = [saved[step, c, at].astype(jnp.float32) for c in range(3)]
            e = [fe[c, at_full, middle] for c in range(3)]
            term = (e[0] * s[0] + e[1] * s[1]) + e[2] * s[2]
            scaled[at] = term if step == 0 else scaled[at] + term

    for c in range(3):
        e_out[c] = fe[c, inner, middle]
        h_out[c] = fh[c, inner, middle] * (1.0 / courant)
    scaled[...] = scaled[...] * inverse[...]
    head, tail = scaled[:RADIUS], scaled[rows - RADIUS :]
    to_a[...] = jnp.where(even_x, tail, head)
    to_b[...] = jnp.where(even_x, head, tail)


def run_steps(electric, magnetic, tensor, saved, xa, xb, ya, yb, ca, cb, inverse):
    rows, width = electric.shape[1:]
    full = (rows + 2 * SUB, width + 2 * SIDE)
    edge = (RADIUS, width)
    return call(
        main_body,
        [electric.shape, magnetic.shape, (rows, width), edge, edge],
        (electric, magnetic, tensor, saved, xa, xb, ya, yb, ca, cb, inverse),
        [pltpu.VMEM((n, *full), jnp.float32) for n in (3, 3, 9)],
        limit=28,
    )


def box(values, unit, axis):
    size = values.shape[axis]

    def ahead(v, places):
        return pltpu.roll(v, size - places * unit, axis)

    two = values + ahead(values, 1)
    four = two + ahead(two, 2)
    eight = four + ahead(four, 4)
    return eight + ahead(values, 8)


def filter_rows(scaled, xa, xb, across, to_a, to_b):
    rows, width = scaled.shape
    even_x, even_y = is_even("gx"), is_even("gy")
    a, b = xa[...], xb[...]
    low, high = jnp.where(even_x, b, a), jnp.where(even_x, a, b)
    extended = jnp.concatenate([low, scaled[...], high], axis=0)
    result = box(box(extended, 1, 0), 1, 0)[:rows] * (1.0 / (RADIUS + 1.0))
    across[...] = result
    head, tail = result[:, :REACH], result[:, width - REACH :]
    to_a[...] = jnp.where(even_y, tail, head)
    to_b[...] = jnp.where(even_y, head, tail)


def filter_columns(across, ya, yb, gradient):
    width = across.shape[1]
    even_y = is_even("gy")
    for r in range(across.shape[0] // SUB):
        at = slice(r * SUB, (r + 1) * SUB)
        a, b = ya[at], yb[at]
        low, high = jnp.where(even_y, b, a), jnp.where(even_y, a, b)
        extended = jnp.concatenate([low, across[at], high], axis=1)
        gradient[at] = box(box(extended, NZ, 1), NZ, 1)[:, :width] * (1.0 / (RADIUS + 1.0))


def tent(offset):
    return (RADIUS + 1.0 - abs(offset)) / (RADIUS + 1.0)


def coverage(places, length):
    total = jnp.zeros(places.shape, jnp.float32)
    for offset in range(-RADIUS, RADIUS + 1):
        inside = ((places + offset >= 0) & (places + offset < length)).astype(jnp.float32)
        total = total + tent(offset) * inside
    return total


def shards(electric, magnetic, tensor, saved):
    rows, width = electric.shape[1:]
    cols = width // NZ
    edge = (RADIUS, width)

    xa, xb = swap(*pack_x(electric, magnetic, tensor), "gx")
    ya, yb = swap(*pack_y(SIDE, electric, magnetic, tensor), "gy")
    ca, cb = swap(*pack_y(SIDE, xa[None], xb[None]), "gy")

    row_places = lax.axis_index("gx") * rows + lax.broadcasted_iota(jnp.int32, (rows, width), 0)
    col_places = lax.axis_index("gy") * cols + lax.broadcasted_iota(jnp.int32, (rows, width), 1) // NZ
    cover = coverage(row_places, lax.axis_size("gx") * rows) * coverage(col_places, lax.axis_size("gy") * cols)

    e, h, scaled, to_a, to_b = run_steps(
        electric, magnetic, tensor, saved, xa, xb, ya, yb, ca, cb, 1.0 / cover
    )
    xa, xb = swap(to_a, to_b, "gx")
    side = (rows, REACH)
    across, to_a, to_b = call(filter_rows, [(rows, width), side, side], (scaled, xa, xb))
    ya, yb = swap(to_a, to_b, "gy")
    (gradient,) = call(filter_columns, [(rows, width)], (across, ya, yb))
    return e, h, gradient


def solution(mesh):
    in_specs = (
        P(None, "gx", "gy"),
        P(None, "gx", "gy"),
        P(None, "gx", "gy"),
        P(None, None, "gx", "gy"),
    )
    out_specs = (P(None, "gx", "gy"), P(None, "gx", "gy"), P("gx", "gy"))
    return jax.shard_map(shards, mesh=mesh, in_specs=in_specs, out_specs=out_specs, check_vma=False)
```

```python
import functools

import jax
import jax.numpy as jnp
from jax import lax
from jax.experimental import pallas as pl
from jax.experimental.pallas import tpu as pltpu
from jax.sharding import PartitionSpec as P


NZ = 48
STEPS = 6
RADIUS = 8
SUB = 8
LANE = 128

courant = 0.45


def up_to(size, unit):
    return -(-size // unit) * unit


HALO = STEPS
SIDE = up_to(HALO * NZ, LANE)
REACH = RADIUS * NZ
AXES = ("gx", "gy")
PACK_LIMIT = 58


def neighbours(axis, other, first, fill):
    count, wide = lax.axis_size(axis), lax.axis_size(other)
    pairs = [((i, j), (i + 1, j)) for i in range(first, count - 1, 2) for j in range(wide)]
    if fill and wide % 2 == 0:
        paired = {i for i, _ in (p for pair in pairs for p in pair)}
        idle = [i for i in range(count) if i not in paired]
        pairs += [((i, j), (i, j + 1)) for i in idle for j in range(0, wide, 2)]
    route = []
    for (i, j), (k, m) in pairs:
        one, two = (i * wide + j, k * wide + m) if axis == AXES[0] else (j * count + i, m * count + k)
        route += [(one, two), (two, one)]
    return route


def swap(to_a, to_b, axis, other, fill=True):
    from_b = lax.ppermute(to_b, AXES, neighbours(axis, other, 1, fill))
    from_a = lax.ppermute(to_a, AXES, neighbours(axis, other, 0, fill))
    return from_a, from_b


def is_even(axis):
    return lax.rem(lax.axis_index(axis), 2) == 0


def sorter(axis):
    index = lax.axis_index(axis)
    even = lax.rem(index, 2) == 0
    starts, ends = index == 0, index == lax.axis_size(axis) - 1

    def low(a, b):
        return jnp.where(starts, 0.0, jnp.where(even, b, a))

    def high(a, b):
        return jnp.where(ends, 0.0, jnp.where(even, a, b))

    return low, high


def call(body, outs, ins, scratch=(), limit=16, aliases=None, cost=2**20):
    vmem = pl.BlockSpec(memory_space=pltpu.VMEM)
    return pl.pallas_call(
        body,
        out_shape=[jax.ShapeDtypeStruct(s, jnp.float32) for s in outs],
        in_specs=[vmem] * len(ins),
        out_specs=[vmem] * len(outs),
        scratch_shapes=list(scratch),
        input_output_aliases=aliases or {},
        cost_estimate=pl.CostEstimate(flops=cost, bytes_accessed=cost, transcendentals=0),
        compiler_params=pltpu.CompilerParams(vmem_limit_bytes=limit * 2**20),
    )(*ins)


FULL = HALO - 1
EXTRA = 3


def columns_of(t, e, row):
    rows = slice(row, row + 1)
    return [
        (t[c, rows] * e[0, rows] + t[3 + c, rows] * e[1, rows]) + t[6 + c, rows] * e[2, rows] for c in range(3)
    ]


def pack_rows(first_e, last_e, first_h, last_h, first_t, last_t, to_a, to_b):
    even = is_even("gx")
    at = 0

    def put(head, tail):
        nonlocal at
        size = head.shape[0]
        to_a[at : at + size, :] = jnp.where(even, tail, head)
        to_b[at : at + size, :] = jnp.where(even, head, tail)
        at += size

    for first, last in ((first_e, last_e), (first_h, last_h), (first_t, last_t)):
        for c in range(first.shape[0]):
            put(first[c, 0:FULL, :], last[c, SUB - FULL : SUB, :])
    ahead = columns_of(first_t, first_e, FULL)
    row = SUB - HALO
    g = columns_of(last_t, last_e, row)
    put(ahead[1], g[0])
    put(ahead[2], last_h[1, row : row + 1] - courant * g[2])
    put(jnp.zeros_like(g[0]), last_h[2, row : row + 1] + courant * g[1])


def pack_x(electric, magnetic, tensor):
    rows, width = electric.shape[1:]
    parts = (electric, magnetic, tensor)
    ins, specs = [], []
    for part in parts:
        for block in (0, rows // SUB - 1):
            ins.append(part)
            specs.append(pl.BlockSpec((part.shape[0], SUB, width), lambda i, block=block: (0, block, 0)))
    packed = FULL * sum(part.shape[0] for part in parts) + EXTRA
    out = jax.ShapeDtypeStruct((packed, width), jnp.float32)
    return pl.pallas_call(
        pack_rows,
        name="pack_x",
        grid=(1,),
        out_shape=[out, out],
        in_specs=specs,
        out_specs=[pl.BlockSpec((packed, width), lambda i: (0, 0))] * 2,
        compiler_params=pltpu.CompilerParams(vmem_limit_bytes=PACK_LIMIT * 2**20),
    )(*ins)


def pack_lanes(size, *refs):
    ins, (to_a, to_b) = refs[:-2], refs[-2:]
    even = is_even("gy")
    at = 0
    for ref in ins:
        width = ref.shape[2]
        for c in range(ref.shape[0]):
            head = ref[c, :, 0:size]
            tail = ref[c, :, width - size : width]
            to_a[at] = jnp.where(even, tail, head)
            to_b[at] = jnp.where(even, head, tail)
            at += 1


def pack_y(size, *ins):
    out = (sum(x.shape[0] for x in ins), ins[0].shape[1], size)
    return call(functools.partial(pack_lanes, size), [out, out], ins)


def place_rows(full_e, full_h, full_t, rows, lanes, low, high):
    fields = [(full_e, c, None) for c in range(3)] + [(full_h, c, courant) for c in range(3)]
    fields += [(full_t, c, courant * courant) for c in range(9)]
    top, bottom = slice(SUB - FULL, SUB), slice(SUB + rows, SUB + rows + FULL)
    for k, (full, c, factor) in enumerate(fields):
        packet = slice(k * FULL, (k + 1) * FULL)
        for at, get in ((top, low), (bottom, high)):
            value = get(packet)
            full[c, at, lanes] = value if factor is None else value * factor
    base = len(fields) * FULL
    extra = [slice(base + i, base + i + 1) for i in range(EXTRA)]
    top, bottom = slice(SUB - HALO, SUB - FULL), slice(SUB + rows + FULL, SUB + rows + HALO)
    full_t[0, top, lanes] = low(extra[0]) * (courant * courant)
    full_h[1, top, lanes] = low(extra[1]) * courant
    full_h[2, top, lanes] = low(extra[2]) * courant
    full_t[1, bottom, lanes] = high(extra[0]) * (courant * courant)
    full_t[2, bottom, lanes] = high(extra[1]) * (courant * courant)
    one = jnp.ones_like(low(extra[0]))
    full_e[0, top, lanes] = one
    full_e[0, bottom, lanes] = one


def assemble_body(e_in, h_in, t_in, xa, xb, ya, yb, fe, fh, ft):
    rows, width = e_in.shape[1:]
    total_rows, total = fe.shape[1:]
    low_x, high_x = sorter("gx")
    low_y, high_y = sorter("gy")
    inner = slice(SUB, SUB + rows)
    middle = slice(SIDE, SIDE + width)
    left, right = slice(0, SIDE), slice(SIDE + width, total)
    top, bottom = slice(0, SUB), slice(SUB + rows, total_rows)
    k = 0
    for own, full, factor in ((e_in, fe, None), (h_in, fh, courant), (t_in, ft, courant * courant)):
        for c in range(own.shape[0]):
            full[c, top, :] = jnp.zeros((SUB, total), jnp.float32)
            full[c, bottom, :] = jnp.zeros((SUB, total), jnp.float32)
            for lanes, value in (
                (middle, own[c]),
                (left, low_y(ya[k], yb[k])),
                (right, high_y(ya[k], yb[k])),
            ):
                full[c, inner, lanes] = value if factor is None else value * factor
            k += 1
    place_rows(fe, fh, ft, rows, middle, lambda s: low_x(xa[s], xb[s]), lambda s: high_x(xa[s], xb[s]))


def main_body(fe_in, fh_in, ft_in, saved, ca, cb, inverse, fe, fh, ft, scaled, to_a, to_b):
    del fe_in, fh_in, ft_in
    rows, width = scaled.shape
    total_rows, total = fe.shape[1:]
    tiles = total_rows // SUB
    middle = slice(SIDE, SIDE + width)
    low_x, high_x = sorter("gx")
    low_y, high_y = sorter("gy")
    even_x = is_even("gx")

    for lanes, side in ((slice(0, SIDE), low_y), (slice(SIDE + width, total), high_y)):

        def of(s, pick, side=side):
            return pick(side(ca[0, s], cb[0, s]), side(ca[1, s], cb[1, s]))

        place_rows(fe, fh, ft, rows, lanes, lambda s, of=of: of(s, low_x), lambda s, of=of: of(s, high_x))

    inside_x = jnp.where(lax.axis_index("gx") > 0, 1.0, 0.0).astype(jnp.float32)
    inside_y = jnp.where(lax.axis_index("gy") > 0, 1.0, 0.0).astype(jnp.float32)

    for step in range(STEPS):
        left_over = STEPS - step
        begin = (SIDE - left_over * NZ) // LANE * LANE
        end = up_to(SIDE + width + left_over * NZ, LANE)
        span = end - begin
        lanes = slice(begin, end)
        sub = lax.broadcasted_iota(jnp.int32, (SUB, span), 0)
        depth = lax.rem(lax.broadcasted_iota(jnp.int32, (SUB, span), 1) + (begin % NZ), NZ)
        upper = (depth != NZ - 1).astype(jnp.float32)
        lower = (depth != 0).astype(jnp.float32)
        low = SIDE - begin
        last = step == STEPS - 1

        def tile(ref, c, r):
            return ref[c, r * SUB : (r + 1) * SUB, lanes]

        def to_tile(ref, c, r, value):
            ref[c, r * SUB : (r + 1) * SUB, lanes] = value

        def from_next_y(f):
            return pltpu.roll(f, span - NZ, 1)

        def from_next_z(f):
            return pltpu.roll(f, span - 1, 1) * upper

        def from_prev_y(f):
            return pltpu.roll(f, NZ, 1)

        def from_prev_z(f):
            return pltpu.roll(f, 1, 1) * lower

        after = None
        for r in reversed(range(tiles)):
            e = [tile(fe, c, r) for c in range(3)]
            g = [
                (tile(ft, c, r) * e[0] + tile(ft, 3 + c, r) * e[1]) + tile(ft, 6 + c, r) * e[2]
                for c in range(3)
            ]
            turned = [None] + [pltpu.roll(g[c], SUB - 1, 0) for c in (1, 2)]
            if after is None:
                after = turned
            if not (last and r == tiles - 1):
                next_x = [None] + [jnp.where(sub == SUB - 1, after[c], turned[c]) for c in (1, 2)]
                curl = [
                    (from_next_y(g[2]) - g[2]) - (from_next_z(g[1]) - g[1]),
                    (from_next_z(g[0]) - g[0]) - (next_x[2] - g[2]),
                    (next_x[1] - g[1]) - (from_next_y(g[0]) - g[0]),
                ]
                for c in range(3):
                    h = tile(fh, c, r) - curl[c]
                    if r == 0:
                        h = h * inside_x
                    h = jnp.concatenate([h[:, :low] * inside_y, h[:, low:]], axis=1)
                    to_tile(fh, c, r, h)
            after = turned

        before = None
        for r in range(tiles):
            if last and r == tiles - 1:
                continue
            h = [tile(fh, c, r) for c in range(3)]
            turned = [None] + [pltpu.roll(h[c], 1, 0) for c in (1, 2)]
            if before is None:
                before = turned
            if not (last and r == 0):
                prev_x = [None] + [jnp.where(sub == 0, before[c], turned[c]) for c in (1, 2)]
                curl = [
                    (h[2] - from_prev_y(h[2])) - (h[1] - from_prev_z(h[1])),
                    (h[0] - from_prev_z(h[0])) - (h[2] - prev_x[2]),
                    (h[1] - prev_x[1]) - (h[0] - from_prev_y(h[0])),
                ]
                for c in range(3):
                    to_tile(fe, c, r, tile(fe, c, r) + curl[c])
            before = turned

        pair = 2 * SUB
        for r in range(rows // pair):
            at = slice(r * pair, (r + 1) * pair)
            at_full = slice(SUB + r * pair, SUB + (r + 1) * pair)
            s = [saved[step, c, at].astype(jnp.float32) for c in range(3)]
            e = [fe[c, at_full, middle] for c in range(3)]
            term = (e[0] * s[0] + e[1] * s[1]) + e[2] * s[2]
            scaled[at] = term if step == 0 else scaled[at] + term

    scaled[...] = scaled[...] * inverse[...]
    head, tail = scaled[:RADIUS], scaled[rows - RADIUS :]
    to_a[...] = jnp.where(even_x, tail, head)
    to_b[...] = jnp.where(even_x, head, tail)


def emit_body(fe, fh, e_out, h_out):
    rows, width = e_out.shape[1:]
    for c in range(3):
        e_out[c] = fe[c, SUB : SUB + rows, SIDE : SIDE + width]
        h_out[c] = fh[c, SUB : SUB + rows, SIDE : SIDE + width] * (1.0 / courant)


def box(values, unit, axis):
    size = values.shape[axis]

    def ahead(v, places):
        return pltpu.roll(v, size - places * unit, axis)

    two = values + ahead(values, 1)
    four = two + ahead(two, 2)
    eight = four + ahead(four, 4)
    return eight + ahead(values, 8)


def filter_rows(scaled, xa, xb, across, to_a, to_b):
    rows, width = scaled.shape
    even_y = is_even("gy")
    low, high = sorter("gx")
    a, b = xa[...], xb[...]
    extended = jnp.concatenate([low(a, b), scaled[...], high(a, b)], axis=0)
    result = box(box(extended, 1, 0), 1, 0)[:rows] * (1.0 / (RADIUS + 1.0))
    across[...] = result
    head, tail = result[:, :REACH], result[:, width - REACH :]
    to_a[...] = jnp.where(even_y, tail, head)
    to_b[...] = jnp.where(even_y, head, tail)


def filter_columns(across, ya, yb, gradient):
    width = across.shape[1]
    low, high = sorter("gy")
    for r in range(across.shape[0] // SUB):
        at = slice(r * SUB, (r + 1) * SUB)
        a, b = ya[at], yb[at]
        extended = jnp.concatenate([low(a, b), across[at], high(a, b)], axis=1)
        gradient[at] = box(box(extended, NZ, 1), NZ, 1)[:, :width] * (1.0 / (RADIUS + 1.0))


def tent(offset):
    return (RADIUS + 1.0 - abs(offset)) / (RADIUS + 1.0)


def coverage(places, length):
    total = jnp.zeros(places.shape, jnp.float32)
    for offset in range(-RADIUS, RADIUS + 1):
        inside = ((places + offset >= 0) & (places + offset < length)).astype(jnp.float32)
        total = total + tent(offset) * inside
    return total


def shards(electric, magnetic, tensor, saved):
    rows, width = electric.shape[1:]
    cols = width // NZ
    edge = (RADIUS, width)
    full = (rows + 2 * SUB, width + 2 * SIDE)
    fulls = [(n, *full) for n in (3, 3, 9)]

    xa, xb = swap(*pack_x(electric, magnetic, tensor), "gx", "gy")
    ya, yb = swap(*pack_y(SIDE, electric, magnetic, tensor), "gy", "gx", fill=False)
    ca, cb = swap(*pack_y(SIDE, xa[None], xb[None]), "gy", "gx")

    row_places = lax.axis_index("gx") * rows + lax.broadcasted_iota(jnp.int32, (rows, width), 0)
    col_places = lax.axis_index("gy") * cols + lax.broadcasted_iota(jnp.int32, (rows, width), 1) // NZ
    cover = coverage(row_places, lax.axis_size("gx") * rows) * coverage(col_places, lax.axis_size("gy") * cols)

    fields = call(assemble_body, fulls, (electric, magnetic, tensor, xa, xb, ya, yb), cost=2**22)
    fe, fh, _, scaled, to_a, to_b = call(
        main_body,
        [*fulls, (rows, width), edge, edge],
        (*fields, saved, ca, cb, 1.0 / cover),
        limit=20,
        aliases={0: 0, 1: 1, 2: 2},
        cost=2**23,
    )
    xa, xb = swap(to_a, to_b, "gx", "gy")
    e, h = call(emit_body, [electric.shape, magnetic.shape], (fe, fh))
    side = (rows, REACH)
    across, to_a, to_b = call(filter_rows, [(rows, width), side, side], (scaled, xa, xb))
    ya, yb = swap(to_a, to_b, "gy", "gx")
    (gradient,) = call(filter_columns, [(rows, width)], (across, ya, yb))
    return e, h, gradient


def solution(mesh):
    in_specs = (
        P(None, "gx", "gy"),
        P(None, "gx", "gy"),
        P(None, "gx", "gy"),
        P(None, None, "gx", "gy"),
    )
    out_specs = (P(None, "gx", "gy"), P(None, "gx", "gy"), P("gx", "gy"))
    return jax.shard_map(shards, mesh=mesh, in_specs=in_specs, out_specs=out_specs, check_vma=False)
```

```python
import jax
import jax.numpy as jnp
from jax import lax
from jax.experimental import pallas as pl
from jax.experimental.pallas import tpu as pltpu
from jax.sharding import PartitionSpec as P


NZ = 48
STEPS = 6
RADIUS = 8
SUB = 8
LANE = 128

courant = 0.45


def up_to(size, unit):
    return -(-size // unit) * unit


HALO = STEPS
SIDE = up_to(HALO * NZ, LANE)
WHOLE = HALO * NZ // LANE * LANE
REST = HALO * NZ - WHOLE
PER_TILE = LANE // REST
REACH = RADIUS * NZ
AXES = ("gx", "gy")
PACK_LIMIT = 8


def neighbours(axis, other, first, fill):
    count, wide = lax.axis_size(axis), lax.axis_size(other)
    pairs = [((i, j), (i + 1, j)) for i in range(first, count - 1, 2) for j in range(wide)]
    if fill and wide % 2 == 0:
        paired = {i for i, _ in (p for pair in pairs for p in pair)}
        idle = [i for i in range(count) if i not in paired]
        pairs += [((i, j), (i, j + 1)) for i in idle for j in range(0, wide, 2)]
    route = []
    for (i, j), (k, m) in pairs:
        one, two = (i * wide + j, k * wide + m) if axis == AXES[0] else (j * count + i, m * count + k)
        route += [(one, two), (two, one)]
    return route


def swap(to_a, to_b, axis, other, fill=True):
    from_b = lax.ppermute(to_b, AXES, neighbours(axis, other, 1, fill))
    from_a = lax.ppermute(to_a, AXES, neighbours(axis, other, 0, fill))
    return from_a, from_b


def is_even(axis):
    return lax.rem(lax.axis_index(axis), 2) == 0


def sorter(axis):
    index = lax.axis_index(axis)
    even = lax.rem(index, 2) == 0
    starts, ends = index == 0, index == lax.axis_size(axis) - 1

    def low(a, b):
        return jnp.where(starts, 0.0, jnp.where(even, b, a))

    def high(a, b):
        return jnp.where(ends, 0.0, jnp.where(even, a, b))

    return low, high


def call(body, outs, ins, scratch=(), limit=16, aliases=None, cost=2**20):
    vmem = pl.BlockSpec(memory_space=pltpu.VMEM)
    return pl.pallas_call(
        body,
        out_shape=[jax.ShapeDtypeStruct(s, jnp.float32) for s in outs],
        in_specs=[vmem] * len(ins),
        out_specs=[vmem] * len(outs),
        scratch_shapes=list(scratch),
        input_output_aliases=aliases or {},
        cost_estimate=pl.CostEstimate(flops=cost, bytes_accessed=cost, transcendentals=0),
        compiler_params=pltpu.CompilerParams(vmem_limit_bytes=limit * 2**20),
    )(*ins)


FULL = HALO - 1
EXTRA = 3


def columns_of(t, e, row):
    rows = slice(row, row + 1)
    return [
        (t[c, rows] * e[0, rows] + t[3 + c, rows] * e[1, rows]) + t[6 + c, rows] * e[2, rows] for c in range(3)
    ]


def pack_rows(e_hbm, h_hbm, t_hbm, to_a, to_b, e_rows, h_rows, t_rows, sems):
    rows = e_hbm.shape[1]
    copies = []
    for n, (source, target) in enumerate(((e_hbm, e_rows), (h_hbm, h_rows), (t_hbm, t_rows))):
        for side, begin in enumerate((0, rows - SUB)):
            copies.append(
                pltpu.make_async_copy(source.at[:, begin : begin + SUB, :], target.at[side], sems.at[n, side])
            )
            copies[-1].start()
    for copy in copies:
        copy.wait()
    even = is_even("gx")
    at = 0

    def put(head, tail):
        nonlocal at
        size = head.shape[0]
        to_a[at : at + size, :] = jnp.where(even, tail, head)
        to_b[at : at + size, :] = jnp.where(even, head, tail)
        at += size

    for part in (e_rows, h_rows, t_rows):
        for c in range(part.shape[1]):
            put(part[0, c, 0:FULL, :], part[1, c, SUB - FULL : SUB, :])
    ahead = columns_of(t_rows.at[0], e_rows.at[0], FULL)
    row = SUB - HALO
    g = columns_of(t_rows.at[1], e_rows.at[1], row)
    put(ahead[1], g[0])
    put(ahead[2], h_rows[1, 1, row : row + 1] - courant * g[2])
    put(jnp.zeros_like(g[0]), h_rows[1, 2, row : row + 1] + courant * g[1])
    spare = to_a.shape[0] - at
    nothing = jnp.zeros((spare, to_a.shape[1]), jnp.float32)
    put(nothing, nothing)


def pack_x(electric, magnetic, tensor):
    width = electric.shape[2]
    parts = (electric, magnetic, tensor)
    packed = up_to(FULL * sum(part.shape[0] for part in parts) + EXTRA, 2 * SUB)
    out = jax.ShapeDtypeStruct((packed, width), jnp.float32)
    return pl.pallas_call(
        pack_rows,
        name="pack_x",
        out_shape=[out, out],
        in_specs=[pl.BlockSpec(memory_space=pltpu.HBM)] * 3,
        out_specs=[pl.BlockSpec(memory_space=pltpu.VMEM)] * 2,
        scratch_shapes=[pltpu.VMEM((2, part.shape[0], SUB, width), jnp.float32) for part in parts]
        + [pltpu.SemaphoreType.DMA((3, 2))],
        compiler_params=pltpu.CompilerParams(vmem_limit_bytes=PACK_LIMIT * 2**20),
    )(*parts)


def quarters(parts):
    slot = lax.broadcasted_iota(jnp.int32, parts[0][0].shape, 1) // REST
    result = None
    for n, (part, first) in enumerate(parts):
        turn = (n * REST - first) % LANE
        turned = pltpu.roll(part, turn, 1) if turn else part
        result = turned if result is None else jnp.where(slot == n, turned, result)
    return result


def whole_and_rest(width, tail):
    if tail:
        return width - WHOLE, width - WHOLE - LANE, LANE - REST
    return 0, WHOLE, 0


def pack_lanes(e_in, h_in, t_in, to_a, to_b):
    even = is_even("gy")
    width = e_in.shape[2]
    fields = [ref.at[c] for ref in (e_in, h_in, t_in) for c in range(ref.shape[0])]
    made = []
    for tail in (False, True):
        whole, rest, first = whole_and_rest(width, tail)
        blocks = [f[:, whole : whole + WHOLE] for f in fields]
        for n in range(0, len(fields), PER_TILE):
            blocks.append(quarters([(f[:, rest : rest + LANE], first) for f in fields[n : n + PER_TILE]]))
        made.append(blocks)
    count = len(fields)
    for k, (head, tail) in enumerate(zip(*made)):
        if k < count:
            at, lanes = k, slice(0, WHOLE)
        else:
            at, half = count + (k - count) // 2, (k - count) % 2
            lanes = slice(half * LANE, (half + 1) * LANE)
        to_a[at, :, lanes] = jnp.where(even, tail, head)
        to_b[at, :, lanes] = jnp.where(even, head, tail)


def from_lanes(ref, k, count, tail):
    group, slot = k // PER_TILE, k % PER_TILE
    at, half = count + group // 2, group % 2
    first = LANE - REST if tail else 0
    turn = (first - slot * REST) % LANE
    rest = ref[at, :, half * LANE : (half + 1) * LANE]
    rest = pltpu.roll(rest, turn, 1) if turn else rest
    whole = ref[k]
    return jnp.concatenate([rest, whole] if tail else [whole, rest], axis=1)


def pack_corners(xa, xb, to_a, to_b):
    even = is_even("gy")
    height, width = xa.shape
    half = height // 2
    made = []
    for tail in (False, True):
        whole, rest, first = whole_and_rest(width, tail)
        pieces = [
            (x[at : at + half, rest : rest + LANE], first) for x in (xa, xb) for at in (0, half)
        ]
        made.append((xa[:, whole : whole + WHOLE], xb[:, whole : whole + WHOLE], quarters(pieces)))
    upper = up_to(half // 2, SUB)
    for out, (blocks_even, blocks_odd) in ((to_a, (made[1], made[0])), (to_b, (made[0], made[1]))):
        one, two, rest = (jnp.where(even, p, q) for p, q in zip(blocks_even, blocks_odd))
        out[0:height] = one
        out[height : 2 * height] = two
        out[2 * height : 2 * height + upper, 0:LANE] = rest[:upper]
        out[2 * height : 2 * height + half - upper, LANE:] = rest[upper:]
        if 2 * upper > half:
            out[2 * height + half - upper :, LANE:] = jnp.zeros((2 * upper - half, LANE), jnp.float32)


def from_corners(ref, height, tail):
    half = height // 2
    upper = up_to(half // 2, SUB)
    base = 2 * height
    rest = jnp.concatenate([ref[base : base + upper, 0:LANE], ref[base : base + half - upper, LANE:]], axis=0)
    first = LANE - REST if tail else 0
    result = []
    for n in range(2):
        turned = []
        for m in range(2):
            turn = (first - (2 * n + m) * REST) % LANE
            turned.append(pltpu.roll(rest, turn, 1) if turn else rest)
        rest_n = jnp.concatenate(turned, axis=0)
        whole = ref[n * height : (n + 1) * height]
        result.append(jnp.concatenate([rest_n, whole] if tail else [whole, rest_n], axis=1))
    return result


def place_rows(full_e, full_h, full_t, rows, lanes, low, high):
    fields = [(full_e, c, None) for c in range(3)] + [(full_h, c, courant) for c in range(3)]
    fields += [(full_t, c, courant * courant) for c in range(9)]
    top, bottom = slice(SUB - FULL, SUB), slice(SUB + rows, SUB + rows + FULL)
    for k, (full, c, factor) in enumerate(fields):
        packet = slice(k * FULL, (k + 1) * FULL)
        for at, get in ((top, low), (bottom, high)):
            value = get(packet)
            full[c, at, lanes] = value if factor is None else value * factor
    base = len(fields) * FULL
    extra = [slice(base + i, base + i + 1) for i in range(EXTRA)]
    top, bottom = slice(SUB - HALO, SUB - FULL), slice(SUB + rows + FULL, SUB + rows + HALO)
    full_t[0, top, lanes] = low(extra[0]) * (courant * courant)
    full_h[1, top, lanes] = low(extra[1]) * courant
    full_h[2, top, lanes] = low(extra[2]) * courant
    full_t[1, bottom, lanes] = high(extra[0]) * (courant * courant)
    full_t[2, bottom, lanes] = high(extra[1]) * (courant * courant)
    one = jnp.ones_like(low(extra[0]))
    full_e[0, top, lanes] = one
    full_e[0, bottom, lanes] = one


def assemble_body(e_in, h_in, t_in, xa, xb, ya, yb, fe, fh, ft, masks):
    rows, width = e_in.shape[1:]
    total_rows, total = fe.shape[1:]
    low_x, high_x = sorter("gx")
    low_y, high_y = sorter("gy")
    inner = slice(SUB, SUB + rows)
    middle = slice(SIDE, SIDE + width)
    left, right = slice(0, SIDE), slice(SIDE + width, total)
    top, bottom = slice(0, SUB), slice(SUB + rows, total_rows)
    count = e_in.shape[0] + h_in.shape[0] + t_in.shape[0]
    k = 0
    for own, full, factor in ((e_in, fe, None), (h_in, fh, courant), (t_in, ft, courant * courant)):
        for c in range(own.shape[0]):
            full[c, top, :] = jnp.zeros((SUB, total), jnp.float32)
            full[c, bottom, :] = jnp.zeros((SUB, total), jnp.float32)
            for lanes, value in (
                (middle, own[c]),
                (left, low_y(from_lanes(ya, k, count, True), from_lanes(yb, k, count, True))),
                (right, high_y(from_lanes(ya, k, count, False), from_lanes(yb, k, count, False))),
            ):
                full[c, inner, lanes] = value if factor is None else value * factor
            k += 1
    depth = lax.rem(lax.broadcasted_iota(jnp.int32, (SUB, total), 1) + (NZ - SIDE % NZ), NZ)
    masks[0] = (depth != NZ - 1).astype(jnp.float32)
    masks[1] = (depth != 0).astype(jnp.float32)
    place_rows(fe, fh, ft, rows, middle, lambda s: low_x(xa[s], xb[s]), lambda s: high_x(xa[s], xb[s]))


def main_body(fe_in, fh_in, ft_in, masks, saved, ca, cb, inverse, fe, fh, ft, scaled, to_a, to_b):
    del fe_in, fh_in, ft_in
    rows, width = scaled.shape
    total_rows, total = fe.shape[1:]
    tiles = total_rows // SUB
    middle = slice(SIDE, SIDE + width)
    low_x, high_x = sorter("gx")
    low_y, high_y = sorter("gy")
    even_x = is_even("gx")

    height = up_to(FULL * 15 + EXTRA, 2 * SUB)
    for lanes, side, tail in ((slice(0, SIDE), low_y, True), (slice(SIDE + width, total), high_y, False)):
        packets = [
            side(a, b) for a, b in zip(from_corners(ca, height, tail), from_corners(cb, height, tail))
        ]
        low, high = low_x(*packets), high_x(*packets)
        place_rows(fe, fh, ft, rows, lanes, lambda s, low=low: low[s], lambda s, high=high: high[s])

    inside_x = jnp.where(lax.axis_index("gx") > 0, 1.0, 0.0).astype(jnp.float32)
    inside_y = jnp.where(lax.axis_index("gy") > 0, 1.0, 0.0).astype(jnp.float32)

    for step in range(STEPS):
        left_over = STEPS - step
        begin = (SIDE - left_over * NZ) // LANE * LANE
        end = up_to(SIDE + width + left_over * NZ, LANE)
        span = end - begin
        lanes = slice(begin, end)
        sub = lax.broadcasted_iota(jnp.int32, (SUB, span), 0)
        upper, lower = masks[0, :, lanes], masks[1, :, lanes]
        low = SIDE - begin
        last = step == STEPS - 1

        def tile(ref, c, r):
            return ref[c, r * SUB : (r + 1) * SUB, lanes]

        def to_tile(ref, c, r, value):
            ref[c, r * SUB : (r + 1) * SUB, lanes] = value

        def from_next_y(f):
            return pltpu.roll(f, span - NZ, 1)

        def from_next_z(f):
            return pltpu.roll(f, span - 1, 1) * upper

        def from_prev_y(f):
            return pltpu.roll(f, NZ, 1)

        def from_prev_z(f):
            return pltpu.roll(f, 1, 1) * lower

        after = None
        for r in reversed(range(tiles)):
            e = [tile(fe, c, r) for c in range(3)]
            g = [
                (tile(ft, c, r) * e[0] + tile(ft, 3 + c, r) * e[1]) + tile(ft, 6 + c, r) * e[2]
                for c in range(3)
            ]
            turned = [None] + [pltpu.roll(g[c], SUB - 1, 0) for c in (1, 2)]
            if after is None:
                after = turned
            if not (last and r == tiles - 1):
                next_x = [None] + [jnp.where(sub == SUB - 1, after[c], turned[c]) for c in (1, 2)]
                curl = [
                    (from_next_y(g[2]) - g[2]) - (from_next_z(g[1]) - g[1]),
                    (from_next_z(g[0]) - g[0]) - (next_x[2] - g[2]),
                    (next_x[1] - g[1]) - (from_next_y(g[0]) - g[0]),
                ]
                for c in range(3):
                    h = tile(fh, c, r) - curl[c]
                    if r == 0:
                        h = h * inside_x
                    h = jnp.concatenate([h[:, :low] * inside_y, h[:, low:]], axis=1)
                    to_tile(fh, c, r, h)
            after = turned

        before = None
        for r in range(tiles):
            if last and r == tiles - 1:
                continue
            h = [tile(fh, c, r) for c in range(3)]
            turned = [None] + [pltpu.roll(h[c], 1, 0) for c in (1, 2)]
            if before is None:
                before = turned
            if not (last and r == 0):
                prev_x = [None] + [jnp.where(sub == 0, before[c], turned[c]) for c in (1, 2)]
                curl = [
                    (h[2] - from_prev_y(h[2])) - (h[1] - from_prev_z(h[1])),
                    (h[0] - from_prev_z(h[0])) - (h[2] - prev_x[2]),
                    (h[1] - prev_x[1]) - (h[0] - from_prev_y(h[0])),
                ]
                for c in range(3):
                    to_tile(fe, c, r, tile(fe, c, r) + curl[c])
            before = turned

        pair = 2 * SUB
        for r in range(rows // pair):
            at = slice(r * pair, (r + 1) * pair)
            at_full = slice(SUB + r * pair, SUB + (r + 1) * pair)
            s = [saved[step, c, at].astype(jnp.float32) for c in range(3)]
            e = [fe[c, at_full, middle] for c in range(3)]
            term = (e[0] * s[0] + e[1] * s[1]) + e[2] * s[2]
            scaled[at] = term if step == 0 else scaled[at] + term

    scaled[...] = scaled[...] * inverse[...]
    head, tail = scaled[:RADIUS], scaled[rows - RADIUS :]
    to_a[...] = jnp.where(even_x, tail, head)
    to_b[...] = jnp.where(even_x, head, tail)


def emit_body(fe, fh, e_out, h_out):
    rows, width = e_out.shape[1:]
    for c in range(3):
        e_out[c] = fe[c, SUB : SUB + rows, SIDE : SIDE + width]
        h_out[c] = fh[c, SUB : SUB + rows, SIDE : SIDE + width] * (1.0 / courant)


def box(values, unit, axis):
    size = values.shape[axis]

    def ahead(v, places):
        return pltpu.roll(v, size - places * unit, axis)

    two = values + ahead(values, 1)
    four = two + ahead(two, 2)
    eight = four + ahead(four, 4)
    return eight + ahead(values, 8)


def filter_rows(scaled, xa, xb, across, to_a, to_b):
    rows, width = scaled.shape
    even_y = is_even("gy")
    low, high = sorter("gx")
    a, b = xa[...], xb[...]
    extended = jnp.concatenate([low(a, b), scaled[...], high(a, b)], axis=0)
    result = box(box(extended, 1, 0), 1, 0)[:rows] * (1.0 / (RADIUS + 1.0))
    across[...] = result
    head, tail = result[:, :REACH], result[:, width - REACH :]
    to_a[...] = jnp.where(even_y, tail, head)
    to_b[...] = jnp.where(even_y, head, tail)


def filter_columns(across, ya, yb, gradient):
    width = across.shape[1]
    low, high = sorter("gy")
    for r in range(across.shape[0] // SUB):
        at = slice(r * SUB, (r + 1) * SUB)
        a, b = ya[at], yb[at]
        extended = jnp.concatenate([low(a, b), across[at], high(a, b)], axis=1)
        gradient[at] = box(box(extended, NZ, 1), NZ, 1)[:, :width] * (1.0 / (RADIUS + 1.0))


def tent(offset):
    return (RADIUS + 1.0 - abs(offset)) / (RADIUS + 1.0)


def coverage(places, length):
    total = jnp.zeros(places.shape, jnp.float32)
    for offset in range(-RADIUS, RADIUS + 1):
        inside = ((places + offset >= 0) & (places + offset < length)).astype(jnp.float32)
        total = total + tent(offset) * inside
    return total


def shards(electric, magnetic, tensor, saved):
    rows, width = electric.shape[1:]
    cols = width // NZ
    edge = (RADIUS, width)
    full = (rows + 2 * SUB, width + 2 * SIDE)
    fulls = [(n, *full) for n in (3, 3, 9)]

    xa, xb = swap(*pack_x(electric, magnetic, tensor), "gx", "gy")
    count = electric.shape[0] + magnetic.shape[0] + tensor.shape[0]
    packet = (count + -(-count // (2 * PER_TILE)), rows, WHOLE)
    ya, yb = swap(*call(pack_lanes, [packet, packet], (electric, magnetic, tensor), limit=8), "gy", "gx", fill=False)
    height = xa.shape[0]
    packet = (2 * height + up_to(height // 4, SUB), WHOLE)
    ca, cb = swap(*call(pack_corners, [packet, packet], (xa, xb), limit=8), "gy", "gx")

    row_places = lax.axis_index("gx") * rows + lax.broadcasted_iota(jnp.int32, (rows, width), 0)
    col_places = lax.axis_index("gy") * cols + lax.broadcasted_iota(jnp.int32, (rows, width), 1) // NZ
    cover = coverage(row_places, lax.axis_size("gx") * rows) * coverage(col_places, lax.axis_size("gy") * cols)

    masks = (2, SUB, full[1])
    fields = call(assemble_body, [*fulls, masks], (electric, magnetic, tensor, xa, xb, ya, yb), cost=2**22)
    fe, fh, _, scaled, to_a, to_b = call(
        main_body,
        [*fulls, (rows, width), edge, edge],
        (*fields, saved, ca, cb, 1.0 / cover),
        limit=20,
        aliases={0: 0, 1: 1, 2: 2},
        cost=2**23,
    )
    xa, xb = swap(to_a, to_b, "gx", "gy")
    e, h = call(emit_body, [electric.shape, magnetic.shape], (fe, fh))
    side = (rows, REACH)
    across, to_a, to_b = call(filter_rows, [(rows, width), side, side], (scaled, xa, xb))
    ya, yb = swap(to_a, to_b, "gy", "gx")
    (gradient,) = call(filter_columns, [(rows, width)], (across, ya, yb))
    return e, h, gradient


def solution(mesh):
    in_specs = (
        P(None, "gx", "gy"),
        P(None, "gx", "gy"),
        P(None, "gx", "gy"),
        P(None, None, "gx", "gy"),
    )
    out_specs = (P(None, "gx", "gy"), P(None, "gx", "gy"), P("gx", "gy"))
    return jax.shard_map(shards, mesh=mesh, in_specs=in_specs, out_specs=out_specs, check_vma=False)
```

```python
import jax
import jax.numpy as jnp
from jax import lax
from jax.experimental import pallas as pl
from jax.experimental.pallas import tpu as pltpu
from jax.sharding import PartitionSpec as P


NZ = 48
STEPS = 6
RADIUS = 8
SUB = 8
LANE = 128

courant = 0.45


def up_to(size, unit):
    return -(-size // unit) * unit


HALO = STEPS
SIDE = up_to(HALO * NZ, LANE)
WHOLE = HALO * NZ // LANE * LANE
REST = HALO * NZ - WHOLE
PER_TILE = LANE // REST
REACH = RADIUS * NZ
AXES = ("gx", "gy")
PACK_LIMIT = 8


def neighbours(axis, other, first, fill):
    count, wide = lax.axis_size(axis), lax.axis_size(other)
    pairs = [((i, j), (i + 1, j)) for i in range(first, count - 1, 2) for j in range(wide)]
    if fill and wide % 2 == 0:
        paired = {i for i, _ in (p for pair in pairs for p in pair)}
        idle = [i for i in range(count) if i not in paired]
        pairs += [((i, j), (i, j + 1)) for i in idle for j in range(0, wide, 2)]
    route = []
    for (i, j), (k, m) in pairs:
        one, two = (i * wide + j, k * wide + m) if axis == AXES[0] else (j * count + i, m * count + k)
        route += [(one, two), (two, one)]
    return route


def swap(to_a, to_b, axis, other, fill=True):
    from_b = lax.ppermute(to_b, AXES, neighbours(axis, other, 1, fill))
    from_a = lax.ppermute(to_a, AXES, neighbours(axis, other, 0, fill))
    return from_a, from_b


def is_even(axis):
    return lax.rem(lax.axis_index(axis), 2) == 0


def sorter(axis):
    index = lax.axis_index(axis)
    even = lax.rem(index, 2) == 0
    starts, ends = index == 0, index == lax.axis_size(axis) - 1

    def low(a, b):
        return jnp.where(starts, 0.0, jnp.where(even, b, a))

    def high(a, b):
        return jnp.where(ends, 0.0, jnp.where(even, a, b))

    return low, high


def call(body, outs, ins, scratch=(), limit=16, aliases=None, cost=2**20, far=()):
    vmem = pl.BlockSpec(memory_space=pltpu.VMEM)
    hbm = pl.BlockSpec(memory_space=pltpu.HBM)
    specs = [hbm if n in far else vmem for n in range(len(ins))]
    ins = [pltpu.with_memory_space_constraint(x, pltpu.HBM) if n in far else x for n, x in enumerate(ins)]
    return pl.pallas_call(
        body,
        out_shape=[jax.ShapeDtypeStruct(s, jnp.float32) for s in outs],
        in_specs=specs,
        out_specs=[vmem] * len(outs),
        scratch_shapes=list(scratch),
        input_output_aliases=aliases or {},
        cost_estimate=pl.CostEstimate(flops=cost, bytes_accessed=cost, transcendentals=0),
        compiler_params=pltpu.CompilerParams(vmem_limit_bytes=limit * 2**20),
    )(*ins)


FULL = HALO - 1
EXTRA = 3


def columns_of(t, e, row):
    rows = slice(row, row + 1)
    return [
        (t[c, rows] * e[0, rows] + t[3 + c, rows] * e[1, rows]) + t[6 + c, rows] * e[2, rows] for c in range(3)
    ]


def pack_rows(e_hbm, h_hbm, t_hbm, to_a, to_b, e_rows, h_rows, t_rows, sems):
    rows = e_hbm.shape[1]
    copies = []
    for n, (source, target) in enumerate(((e_hbm, e_rows), (h_hbm, h_rows), (t_hbm, t_rows))):
        for side, begin in enumerate((0, rows - SUB)):
            copies.append(
                pltpu.make_async_copy(source.at[:, begin : begin + SUB, :], target.at[side], sems.at[n, side])
            )
            copies[-1].start()
    for copy in copies:
        copy.wait()
    even = is_even("gx")
    at = 0

    def put(head, tail):
        nonlocal at
        size = head.shape[0]
        to_a[at : at + size, :] = jnp.where(even, tail, head)
        to_b[at : at + size, :] = jnp.where(even, head, tail)
        at += size

    for part in (e_rows, h_rows, t_rows):
        for c in range(part.shape[1]):
            put(part[0, c, 0:FULL, :], part[1, c, SUB - FULL : SUB, :])
    ahead = columns_of(t_rows.at[0], e_rows.at[0], FULL)
    row = SUB - HALO
    g = columns_of(t_rows.at[1], e_rows.at[1], row)
    put(ahead[1], g[0])
    put(ahead[2], h_rows[1, 1, row : row + 1] - courant * g[2])
    put(jnp.zeros_like(g[0]), h_rows[1, 2, row : row + 1] + courant * g[1])
    spare = to_a.shape[0] - at
    nothing = jnp.zeros((spare, to_a.shape[1]), jnp.float32)
    put(nothing, nothing)


def pack_x(electric, magnetic, tensor):
    width = electric.shape[2]
    parts = (electric, magnetic, tensor)
    packed = up_to(FULL * sum(part.shape[0] for part in parts) + EXTRA, 2 * SUB)
    out = jax.ShapeDtypeStruct((packed, width), jnp.float32)
    return pl.pallas_call(
        pack_rows,
        name="pack_x",
        out_shape=[out, out],
        in_specs=[pl.BlockSpec(memory_space=pltpu.HBM)] * 3,
        out_specs=[pl.BlockSpec(memory_space=pltpu.VMEM)] * 2,
        scratch_shapes=[pltpu.VMEM((2, part.shape[0], SUB, width), jnp.float32) for part in parts]
        + [pltpu.SemaphoreType.DMA((3, 2))],
        compiler_params=pltpu.CompilerParams(vmem_limit_bytes=PACK_LIMIT * 2**20),
    )(*(pltpu.with_memory_space_constraint(part, pltpu.HBM) for part in parts))


def fetch(sources, targets, sems):
    copies = [pltpu.make_async_copy(s, t, sems.at[n]) for n, (s, t) in enumerate(zip(sources, targets))]
    for copy in copies:
        copy.start()
    return copies


def room(*arrays):
    return [pltpu.VMEM(x.shape, x.dtype) for x in arrays] + [pltpu.SemaphoreType.DMA((len(arrays),))]


def quarters(parts):
    slot = lax.broadcasted_iota(jnp.int32, parts[0][0].shape, 1) // REST
    result = None
    for n, (part, first) in enumerate(parts):
        turn = (n * REST - first) % LANE
        turned = pltpu.roll(part, turn, 1) if turn else part
        result = turned if result is None else jnp.where(slot == n, turned, result)
    return result


def whole_and_rest(width, tail):
    if tail:
        return width - WHOLE, width - WHOLE - LANE, LANE - REST
    return 0, WHOLE, 0


def pack_lanes(e_far, h_far, t_far, to_a, to_b, e_in, h_in, t_in, sems):
    for copy in fetch((e_far, h_far, t_far), (e_in, h_in, t_in), sems):
        copy.wait()
    even = is_even("gy")
    width = e_in.shape[2]
    fields = [ref.at[c] for ref in (e_in, h_in, t_in) for c in range(ref.shape[0])]
    made = []
    for tail in (False, True):
        whole, rest, first = whole_and_rest(width, tail)
        blocks = [f[:, whole : whole + WHOLE] for f in fields]
        for n in range(0, len(fields), PER_TILE):
            blocks.append(quarters([(f[:, rest : rest + LANE], first) for f in fields[n : n + PER_TILE]]))
        made.append(blocks)
    count = len(fields)
    for k, (head, tail) in enumerate(zip(*made)):
        if k < count:
            at, lanes = k, slice(0, WHOLE)
        else:
            at, half = count + (k - count) // 2, (k - count) % 2
            lanes = slice(half * LANE, (half + 1) * LANE)
        to_a[at, :, lanes] = jnp.where(even, tail, head)
        to_b[at, :, lanes] = jnp.where(even, head, tail)


def from_lanes(ref, k, count, tail):
    group, slot = k // PER_TILE, k % PER_TILE
    at, half = count + group // 2, group % 2
    first = LANE - REST if tail else 0
    turn = (first - slot * REST) % LANE
    rest = ref[at, :, half * LANE : (half + 1) * LANE]
    rest = pltpu.roll(rest, turn, 1) if turn else rest
    whole = ref[k]
    return jnp.concatenate([rest, whole] if tail else [whole, rest], axis=1)


def pack_corners(xa, xb, to_a, to_b):
    even = is_even("gy")
    height, width = xa.shape
    half = height // 2
    made = []
    for tail in (False, True):
        whole, rest, first = whole_and_rest(width, tail)
        pieces = [
            (x[at : at + half, rest : rest + LANE], first) for x in (xa, xb) for at in (0, half)
        ]
        made.append((xa[:, whole : whole + WHOLE], xb[:, whole : whole + WHOLE], quarters(pieces)))
    upper = up_to(half // 2, SUB)
    for out, (blocks_even, blocks_odd) in ((to_a, (made[1], made[0])), (to_b, (made[0], made[1]))):
        one, two, rest = (jnp.where(even, p, q) for p, q in zip(blocks_even, blocks_odd))
        out[0:height] = one
        out[height : 2 * height] = two
        out[2 * height : 2 * height + upper, 0:LANE] = rest[:upper]
        out[2 * height : 2 * height + half - upper, LANE:] = rest[upper:]
        if 2 * upper > half:
            out[2 * height + half - upper :, LANE:] = jnp.zeros((2 * upper - half, LANE), jnp.float32)


def from_corners(ref, height, tail):
    half = height // 2
    upper = up_to(half // 2, SUB)
    base = 2 * height
    rest = jnp.concatenate([ref[base : base + upper, 0:LANE], ref[base : base + half - upper, LANE:]], axis=0)
    first = LANE - REST if tail else 0
    result = []
    for n in range(2):
        turned = []
        for m in range(2):
            turn = (first - (2 * n + m) * REST) % LANE
            turned.append(pltpu.roll(rest, turn, 1) if turn else rest)
        rest_n = jnp.concatenate(turned, axis=0)
        whole = ref[n * height : (n + 1) * height]
        result.append(jnp.concatenate([rest_n, whole] if tail else [whole, rest_n], axis=1))
    return result


def place_rows(full_e, full_h, full_t, rows, lanes, low, high):
    fields = [(full_e, c, None) for c in range(3)] + [(full_h, c, courant) for c in range(3)]
    fields += [(full_t, c, courant * courant) for c in range(9)]
    top, bottom = slice(SUB - FULL, SUB), slice(SUB + rows, SUB + rows + FULL)
    for k, (full, c, factor) in enumerate(fields):
        packet = slice(k * FULL, (k + 1) * FULL)
        for at, get in ((top, low), (bottom, high)):
            value = get(packet)
            full[c, at, lanes] = value if factor is None else value * factor
    base = len(fields) * FULL
    extra = [slice(base + i, base + i + 1) for i in range(EXTRA)]
    top, bottom = slice(SUB - HALO, SUB - FULL), slice(SUB + rows + FULL, SUB + rows + HALO)
    full_t[0, top, lanes] = low(extra[0]) * (courant * courant)
    full_h[1, top, lanes] = low(extra[1]) * courant
    full_h[2, top, lanes] = low(extra[2]) * courant
    full_t[1, bottom, lanes] = high(extra[0]) * (courant * courant)
    full_t[2, bottom, lanes] = high(extra[1]) * (courant * courant)
    one = jnp.ones_like(low(extra[0]))
    full_e[0, top, lanes] = one
    full_e[0, bottom, lanes] = one


def assemble_body(e_far, h_far, t_far, xa, xb, ya, yb, fe, fh, ft, masks, e_in, h_in, t_in, sems):
    copies = fetch((e_far, h_far, t_far), (e_in, h_in, t_in), sems)
    rows, width = e_in.shape[1:]
    total_rows, total = fe.shape[1:]
    low_x, high_x = sorter("gx")
    low_y, high_y = sorter("gy")
    inner = slice(SUB, SUB + rows)
    middle = slice(SIDE, SIDE + width)
    left, right = slice(0, SIDE), slice(SIDE + width, total)
    top, bottom = slice(0, SUB), slice(SUB + rows, total_rows)
    count = e_in.shape[0] + h_in.shape[0] + t_in.shape[0]
    fields = []
    for own, full, factor in ((e_in, fe, None), (h_in, fh, courant), (t_in, ft, courant * courant)):
        fields += [(own, full, factor, c) for c in range(own.shape[0])]

    def scaled_to(factor, value):
        return value if factor is None else value * factor

    for k, (own, full, factor, c) in enumerate(fields):
        full[c, top, :] = jnp.zeros((SUB, total), jnp.float32)
        full[c, bottom, :] = jnp.zeros((SUB, total), jnp.float32)
        for lanes, side, tail in ((left, low_y, True), (right, high_y, False)):
            value = side(from_lanes(ya, k, count, tail), from_lanes(yb, k, count, tail))
            full[c, inner, lanes] = scaled_to(factor, value)
    depth = lax.rem(lax.broadcasted_iota(jnp.int32, (SUB, total), 1) + (NZ - SIDE % NZ), NZ)
    masks[0] = (depth != NZ - 1).astype(jnp.float32)
    masks[1] = (depth != 0).astype(jnp.float32)
    place_rows(fe, fh, ft, rows, middle, lambda s: low_x(xa[s], xb[s]), lambda s: high_x(xa[s], xb[s]))
    for copy in copies:
        copy.wait()
    for own, full, factor, c in fields:
        full[c, inner, middle] = scaled_to(factor, own[c])


def main_body(fe_in, fh_in, ft_in, masks, s_far, ca, cb, inverse, fe, fh, ft, scaled, to_a, to_b, saved, sems):
    del fe_in, fh_in, ft_in
    (frames,) = fetch((s_far,), (saved,), sems)
    rows, width = scaled.shape
    total_rows, total = fe.shape[1:]
    tiles = total_rows // SUB
    middle = slice(SIDE, SIDE + width)
    low_x, high_x = sorter("gx")
    low_y, high_y = sorter("gy")
    even_x = is_even("gx")

    height = up_to(FULL * 15 + EXTRA, 2 * SUB)
    for lanes, side, tail in ((slice(0, SIDE), low_y, True), (slice(SIDE + width, total), high_y, False)):
        packets = [
            side(a, b) for a, b in zip(from_corners(ca, height, tail), from_corners(cb, height, tail))
        ]
        low, high = low_x(*packets), high_x(*packets)
        place_rows(fe, fh, ft, rows, lanes, lambda s, low=low: low[s], lambda s, high=high: high[s])

    inside_x = jnp.where(lax.axis_index("gx") > 0, 1.0, 0.0).astype(jnp.float32)
    inside_y = jnp.where(lax.axis_index("gy") > 0, 1.0, 0.0).astype(jnp.float32)

    for step in range(STEPS):
        left_over = STEPS - step
        begin = (SIDE - left_over * NZ) // LANE * LANE
        end = up_to(SIDE + width + left_over * NZ, LANE)
        span = end - begin
        lanes = slice(begin, end)
        sub = lax.broadcasted_iota(jnp.int32, (SUB, span), 0)
        upper, lower = masks[0, :, lanes], masks[1, :, lanes]
        low = SIDE - begin
        last = step == STEPS - 1

        def tile(ref, c, r):
            return ref[c, r * SUB : (r + 1) * SUB, lanes]

        def to_tile(ref, c, r, value):
            ref[c, r * SUB : (r + 1) * SUB, lanes] = value

        def from_next_y(f):
            return pltpu.roll(f, span - NZ, 1)

        def from_next_z(f):
            return pltpu.roll(f, span - 1, 1) * upper

        def from_prev_y(f):
            return pltpu.roll(f, NZ, 1)

        def from_prev_z(f):
            return pltpu.roll(f, 1, 1) * lower

        after = None
        for r in reversed(range(tiles)):
            e = [tile(fe, c, r) for c in range(3)]
            g = [
                (tile(ft, c, r) * e[0] + tile(ft, 3 + c, r) * e[1]) + tile(ft, 6 + c, r) * e[2]
                for c in range(3)
            ]
            turned = [None] + [pltpu.roll(g[c], SUB - 1, 0) for c in (1, 2)]
            if after is None:
                after = turned
            if not (last and r == tiles - 1):
                next_x = [None] + [jnp.where(sub == SUB - 1, after[c], turned[c]) for c in (1, 2)]
                curl = [
                    (from_next_y(g[2]) - g[2]) - (from_next_z(g[1]) - g[1]),
                    (from_next_z(g[0]) - g[0]) - (next_x[2] - g[2]),
                    (next_x[1] - g[1]) - (from_next_y(g[0]) - g[0]),
                ]
                for c in range(3):
                    h = tile(fh, c, r) - curl[c]
                    if r == 0:
                        h = h * inside_x
                    h = jnp.concatenate([h[:, :low] * inside_y, h[:, low:]], axis=1)
                    to_tile(fh, c, r, h)
            after = turned

        before = None
        for r in range(tiles):
            if last and r == tiles - 1:
                continue
            h = [tile(fh, c, r) for c in range(3)]
            turned = [None] + [pltpu.roll(h[c], 1, 0) for c in (1, 2)]
            if before is None:
                before = turned
            if not (last and r == 0):
                prev_x = [None] + [jnp.where(sub == 0, before[c], turned[c]) for c in (1, 2)]
                curl = [
                    (h[2] - from_prev_y(h[2])) - (h[1] - from_prev_z(h[1])),
                    (h[0] - from_prev_z(h[0])) - (h[2] - prev_x[2]),
                    (h[1] - prev_x[1]) - (h[0] - from_prev_y(h[0])),
                ]
                for c in range(3):
                    to_tile(fe, c, r, tile(fe, c, r) + curl[c])
            before = turned

        if step == 0:
            frames.wait()
        pair = 2 * SUB
        for r in range(rows // pair):
            at = slice(r * pair, (r + 1) * pair)
            at_full = slice(SUB + r * pair, SUB + (r + 1) * pair)
            s = [saved[step, c, at].astype(jnp.float32) for c in range(3)]
            e = [fe[c, at_full, middle] for c in range(3)]
            term = (e[0] * s[0] + e[1] * s[1]) + e[2] * s[2]
            scaled[at] = term if step == 0 else scaled[at] + term

    scaled[...] = scaled[...] * inverse[...]
    head, tail = scaled[:RADIUS], scaled[rows - RADIUS :]
    to_a[...] = jnp.where(even_x, tail, head)
    to_b[...] = jnp.where(even_x, head, tail)


def emit_body(fe, fh, e_out, h_out):
    rows, width = e_out.shape[1:]
    for c in range(3):
        e_out[c] = fe[c, SUB : SUB + rows, SIDE : SIDE + width]
        h_out[c] = fh[c, SUB : SUB + rows, SIDE : SIDE + width] * (1.0 / courant)


def box(values, unit, axis):
    size = values.shape[axis]

    def ahead(v, places):
        return pltpu.roll(v, size - places * unit, axis)

    two = values + ahead(values, 1)
    four = two + ahead(two, 2)
    eight = four + ahead(four, 4)
    return eight + ahead(values, 8)


def filter_rows(scaled, xa, xb, across, to_a, to_b):
    rows, width = scaled.shape
    even_y = is_even("gy")
    low, high = sorter("gx")
    a, b = xa[...], xb[...]
    extended = jnp.concatenate([low(a, b), scaled[...], high(a, b)], axis=0)
    result = box(box(extended, 1, 0), 1, 0)[:rows] * (1.0 / (RADIUS + 1.0))
    across[...] = result
    head, tail = result[:, :REACH], result[:, width - REACH :]
    to_a[...] = jnp.where(even_y, tail, head)
    to_b[...] = jnp.where(even_y, head, tail)


def filter_columns(across, ya, yb, gradient):
    width = across.shape[1]
    low, high = sorter("gy")
    for r in range(across.shape[0] // SUB):
        at = slice(r * SUB, (r + 1) * SUB)
        a, b = ya[at], yb[at]
        extended = jnp.concatenate([low(a, b), across[at], high(a, b)], axis=1)
        gradient[at] = box(box(extended, NZ, 1), NZ, 1)[:, :width] * (1.0 / (RADIUS + 1.0))


def tent(offset):
    return (RADIUS + 1.0 - abs(offset)) / (RADIUS + 1.0)


def coverage(places, length):
    total = jnp.zeros(places.shape, jnp.float32)
    for offset in range(-RADIUS, RADIUS + 1):
        inside = ((places + offset >= 0) & (places + offset < length)).astype(jnp.float32)
        total = total + tent(offset) * inside
    return total


def shards(electric, magnetic, tensor, saved):
    rows, width = electric.shape[1:]
    cols = width // NZ
    edge = (RADIUS, width)
    full = (rows + 2 * SUB, width + 2 * SIDE)
    fulls = [(n, *full) for n in (3, 3, 9)]

    own = (electric, magnetic, tensor)
    xa, xb = swap(*pack_x(electric, magnetic, tensor), "gx", "gy")
    count = electric.shape[0] + magnetic.shape[0] + tensor.shape[0]
    packet = (count + -(-count // (2 * PER_TILE)), rows, WHOLE)
    ya, yb = swap(*call(pack_lanes, [packet, packet], own, room(*own), limit=8, far=(0, 1, 2)), "gy", "gx", fill=False)
    height = xa.shape[0]
    packet = (2 * height + up_to(height // 4, SUB), WHOLE)
    ca, cb = swap(*call(pack_corners, [packet, packet], (xa, xb), limit=8), "gy", "gx")

    row_places = lax.axis_index("gx") * rows + lax.broadcasted_iota(jnp.int32, (rows, width), 0)
    col_places = lax.axis_index("gy") * cols + lax.broadcasted_iota(jnp.int32, (rows, width), 1) // NZ
    cover = coverage(row_places, lax.axis_size("gx") * rows) * coverage(col_places, lax.axis_size("gy") * cols)

    masks = (2, SUB, full[1])
    fields = call(assemble_body, [*fulls, masks], (*own, xa, xb, ya, yb), room(*own), cost=2**22, far=(0, 1, 2))
    fe, fh, _, scaled, to_a, to_b = call(
        main_body,
        [*fulls, (rows, width), edge, edge],
        (*fields, saved, ca, cb, 1.0 / cover),
        room(saved),
        limit=20,
        far=(4,),
        aliases={0: 0, 1: 1, 2: 2},
        cost=2**23,
    )
    xa, xb = swap(to_a, to_b, "gx", "gy")
    e, h = call(emit_body, [electric.shape, magnetic.shape], (fe, fh))
    side = (rows, REACH)
    across, to_a, to_b = call(filter_rows, [(rows, width), side, side], (scaled, xa, xb))
    ya, yb = swap(to_a, to_b, "gy", "gx")
    (gradient,) = call(filter_columns, [(rows, width)], (across, ya, yb))
    return e, h, gradient


def solution(mesh):
    in_specs = (
        P(None, "gx", "gy"),
        P(None, "gx", "gy"),
        P(None, "gx", "gy"),
        P(None, None, "gx", "gy"),
    )
    out_specs = (P(None, "gx", "gy"), P(None, "gx", "gy"), P("gx", "gy"))
    return jax.shard_map(shards, mesh=mesh, in_specs=in_specs, out_specs=out_specs, check_vma=False)
```

```python
import math

import jax
import jax.numpy as jnp
from jax import lax
from jax.experimental import pallas as pl
from jax.experimental.pallas import tpu as pltpu
from jax.sharding import PartitionSpec as P


NZ = 48
STEPS = 6
RADIUS = 8
SUB = 8
LANE = 128

courant = 0.45


def up_to(size, unit):
    return -(-size // unit) * unit


HALO = STEPS
SIDE = up_to(HALO * NZ, LANE)
WHOLE = HALO * NZ // LANE * LANE
REST = HALO * NZ - WHOLE
PER_TILE = LANE // REST
REACH = RADIUS * NZ
AXES = ("gx", "gy")
PACK_LIMIT = 8


def neighbours(axis, other, first, fill):
    count, wide = lax.axis_size(axis), lax.axis_size(other)
    pairs = [((i, j), (i + 1, j)) for i in range(first, count - 1, 2) for j in range(wide)]
    if fill and wide % 2 == 0:
        paired = {i for i, _ in (p for pair in pairs for p in pair)}
        idle = [i for i in range(count) if i not in paired]
        pairs += [((i, j), (i, j + 1)) for i in idle for j in range(0, wide, 2)]
    route = []
    for (i, j), (k, m) in pairs:
        one, two = (i * wide + j, k * wide + m) if axis == AXES[0] else (j * count + i, m * count + k)
        route += [(one, two), (two, one)]
    return route


def swap(to_a, to_b, axis, other, fill=True):
    from_b = lax.ppermute(to_b, AXES, neighbours(axis, other, 1, fill))
    from_a = lax.ppermute(to_a, AXES, neighbours(axis, other, 0, fill))
    return from_a, from_b


def is_even(axis):
    return lax.rem(lax.axis_index(axis), 2) == 0


def sorter(axis):
    index = lax.axis_index(axis)
    even = lax.rem(index, 2) == 0
    starts, ends = index == 0, index == lax.axis_size(axis) - 1

    def low(a, b):
        return jnp.where(starts, 0.0, jnp.where(even, b, a))

    def high(a, b):
        return jnp.where(ends, 0.0, jnp.where(even, a, b))

    return low, high


def call(body, outs, ins, scratch=(), limit=16, aliases=None, cost=2**20, far=()):
    vmem = pl.BlockSpec(memory_space=pltpu.VMEM)
    hbm = pl.BlockSpec(memory_space=pltpu.HBM)
    specs = [hbm if n in far else vmem for n in range(len(ins))]
    ins = [pltpu.with_memory_space_constraint(x, pltpu.HBM) if n in far else x for n, x in enumerate(ins)]
    return pl.pallas_call(
        body,
        out_shape=[jax.ShapeDtypeStruct(s, jnp.float32) for s in outs],
        in_specs=specs,
        out_specs=[vmem] * len(outs),
        scratch_shapes=list(scratch),
        input_output_aliases=aliases or {},
        cost_estimate=pl.CostEstimate(flops=cost, bytes_accessed=cost, transcendentals=0),
        compiler_params=pltpu.CompilerParams(vmem_limit_bytes=limit * 2**20),
    )(*ins)


FULL = HALO - 1
EXTRA = 3


def columns_of(t, e, row):
    rows = slice(row, row + 1)
    return [
        (t[c, rows] * e[0, rows] + t[3 + c, rows] * e[1, rows]) + t[6 + c, rows] * e[2, rows] for c in range(3)
    ]


def pack_rows(e_hbm, h_hbm, t_hbm, to_a, to_b, e_rows, h_rows, t_rows, sems):
    rows = e_hbm.shape[1]
    copies = []
    for n, (source, target) in enumerate(((e_hbm, e_rows), (h_hbm, h_rows), (t_hbm, t_rows))):
        for side, begin in enumerate((0, rows - SUB)):
            copies.append(
                pltpu.make_async_copy(source.at[:, begin : begin + SUB, :], target.at[side], sems.at[n, side])
            )
            copies[-1].start()
    for copy in copies:
        copy.wait()
    even = is_even("gx")
    at = 0

    def put(head, tail):
        nonlocal at
        size = head.shape[0]
        to_a[at : at + size, :] = jnp.where(even, tail, head)
        to_b[at : at + size, :] = jnp.where(even, head, tail)
        at += size

    for part in (e_rows, h_rows, t_rows):
        for c in range(part.shape[1]):
            put(part[0, c, 0:FULL, :], part[1, c, SUB - FULL : SUB, :])
    ahead = columns_of(t_rows.at[0], e_rows.at[0], FULL)
    row = SUB - HALO
    g = columns_of(t_rows.at[1], e_rows.at[1], row)
    put(ahead[1], g[0])
    put(ahead[2], h_rows[1, 1, row : row + 1] - courant * g[2])
    put(jnp.zeros_like(g[0]), h_rows[1, 2, row : row + 1] + courant * g[1])
    spare = to_a.shape[0] - at
    nothing = jnp.zeros((spare, to_a.shape[1]), jnp.float32)
    put(nothing, nothing)


def pack_x(electric, magnetic, tensor):
    width = electric.shape[2]
    parts = (electric, magnetic, tensor)
    packed = up_to(FULL * sum(part.shape[0] for part in parts) + EXTRA, 2 * SUB)
    out = jax.ShapeDtypeStruct((packed, width), jnp.float32)
    return pl.pallas_call(
        pack_rows,
        name="pack_x",
        out_shape=[out, out],
        in_specs=[pl.BlockSpec(memory_space=pltpu.HBM)] * 3,
        out_specs=[pl.BlockSpec(memory_space=pltpu.VMEM)] * 2,
        scratch_shapes=[pltpu.VMEM((2, part.shape[0], SUB, width), jnp.float32) for part in parts]
        + [pltpu.SemaphoreType.DMA((3, 2))],
        compiler_params=pltpu.CompilerParams(vmem_limit_bytes=PACK_LIMIT * 2**20),
    )(*(pltpu.with_memory_space_constraint(part, pltpu.HBM) for part in parts))


def fetch(sources, targets, sems):
    copies = [pltpu.make_async_copy(s, t, sems.at[n]) for n, (s, t) in enumerate(zip(sources, targets))]
    for copy in copies:
        copy.start()
    return copies


def room(*arrays):
    return [pltpu.VMEM(x.shape, x.dtype) for x in arrays] + [pltpu.SemaphoreType.DMA((len(arrays),))]


def quarters(parts):
    slot = lax.broadcasted_iota(jnp.int32, parts[0][0].shape, 1) // REST
    result = None
    for n, (part, first) in enumerate(parts):
        turn = (n * REST - first) % LANE
        turned = pltpu.roll(part, turn, 1) if turn else part
        result = turned if result is None else jnp.where(slot == n, turned, result)
    return result


def whole_and_rest(width, tail):
    if tail:
        return width - WHOLE, width - WHOLE - LANE, LANE - REST
    return 0, WHOLE, 0


def pack_lanes(e_far, h_far, t_far, to_a, to_b, e_in, h_in, t_in, sems):
    for copy in fetch((e_far, h_far, t_far), (e_in, h_in, t_in), sems):
        copy.wait()
    even = is_even("gy")
    width = e_in.shape[2]
    fields = [ref.at[c] for ref in (e_in, h_in, t_in) for c in range(ref.shape[0])]
    made = []
    for tail in (False, True):
        whole, rest, first = whole_and_rest(width, tail)
        blocks = [f[:, whole : whole + WHOLE] for f in fields]
        for n in range(0, len(fields), PER_TILE):
            blocks.append(quarters([(f[:, rest : rest + LANE], first) for f in fields[n : n + PER_TILE]]))
        made.append(blocks)
    count = len(fields)
    for k, (head, tail) in enumerate(zip(*made)):
        if k < count:
            at, lanes = k, slice(0, WHOLE)
        else:
            at, half = count + (k - count) // 2, (k - count) % 2
            lanes = slice(half * LANE, (half + 1) * LANE)
        to_a[at, :, lanes] = jnp.where(even, tail, head)
        to_b[at, :, lanes] = jnp.where(even, head, tail)


def from_lanes(ref, k, count, tail):
    group, slot = k // PER_TILE, k % PER_TILE
    at, half = count + group // 2, group % 2
    first = LANE - REST if tail else 0
    turn = (first - slot * REST) % LANE
    rest = ref[at, :, half * LANE : (half + 1) * LANE]
    rest = pltpu.roll(rest, turn, 1) if turn else rest
    whole = ref[k]
    return jnp.concatenate([rest, whole] if tail else [whole, rest], axis=1)


def pack_corners(xa, xb, to_a, to_b):
    even = is_even("gy")
    height, width = xa.shape
    half = height // 2
    made = []
    for tail in (False, True):
        whole, rest, first = whole_and_rest(width, tail)
        pieces = [
            (x[at : at + half, rest : rest + LANE], first) for x in (xa, xb) for at in (0, half)
        ]
        made.append((xa[:, whole : whole + WHOLE], xb[:, whole : whole + WHOLE], quarters(pieces)))
    upper = up_to(half // 2, SUB)
    for out, (blocks_even, blocks_odd) in ((to_a, (made[1], made[0])), (to_b, (made[0], made[1]))):
        one, two, rest = (jnp.where(even, p, q) for p, q in zip(blocks_even, blocks_odd))
        out[0:height] = one
        out[height : 2 * height] = two
        out[2 * height : 2 * height + upper, 0:LANE] = rest[:upper]
        out[2 * height : 2 * height + half - upper, LANE:] = rest[upper:]
        if 2 * upper > half:
            out[2 * height + half - upper :, LANE:] = jnp.zeros((2 * upper - half, LANE), jnp.float32)


def from_corners(ref, height, tail):
    half = height // 2
    upper = up_to(half // 2, SUB)
    base = 2 * height
    rest = jnp.concatenate([ref[base : base + upper, 0:LANE], ref[base : base + half - upper, LANE:]], axis=0)
    first = LANE - REST if tail else 0
    result = []
    for n in range(2):
        turned = []
        for m in range(2):
            turn = (first - (2 * n + m) * REST) % LANE
            turned.append(pltpu.roll(rest, turn, 1) if turn else rest)
        rest_n = jnp.concatenate(turned, axis=0)
        whole = ref[n * height : (n + 1) * height]
        result.append(jnp.concatenate([rest_n, whole] if tail else [whole, rest_n], axis=1))
    return result


def put(full, c, rows, begin, value):
    for n in range(value.shape[1] // LANE):
        full[c, begin // LANE + n, rows, :] = value[:, n * LANE : (n + 1) * LANE]


def place_rows(full_e, full_h, full_t, rows, begin, low, high):
    fields = [(full_e, c, None) for c in range(3)] + [(full_h, c, courant) for c in range(3)]
    fields += [(full_t, c, courant * courant) for c in range(9)]
    top, bottom = slice(SUB - FULL, SUB), slice(SUB + rows, SUB + rows + FULL)
    for k, (full, c, factor) in enumerate(fields):
        packet = slice(k * FULL, (k + 1) * FULL)
        for at, get in ((top, low), (bottom, high)):
            value = get(packet)
            put(full, c, at, begin, value if factor is None else value * factor)
    base = len(fields) * FULL
    extra = [slice(base + i, base + i + 1) for i in range(EXTRA)]
    top, bottom = slice(SUB - HALO, SUB - FULL), slice(SUB + rows + FULL, SUB + rows + HALO)
    put(full_t, 0, top, begin, low(extra[0]) * (courant * courant))
    put(full_h, 1, top, begin, low(extra[1]) * courant)
    put(full_h, 2, top, begin, low(extra[2]) * courant)
    put(full_t, 1, bottom, begin, high(extra[0]) * (courant * courant))
    put(full_t, 2, bottom, begin, high(extra[1]) * (courant * courant))
    one = jnp.ones_like(low(extra[0]))
    put(full_e, 0, top, begin, one)
    put(full_e, 0, bottom, begin, one)


def assemble_body(e_far, h_far, t_far, xa, xb, ya, yb, fe, fh, ft, e_in, h_in, t_in, sems):
    copies = fetch((e_far, h_far, t_far), (e_in, h_in, t_in), sems)
    rows, width = e_in.shape[1:]
    total_rows = fe.shape[2]
    low_x, high_x = sorter("gx")
    low_y, high_y = sorter("gy")
    inner, top, bottom = slice(SUB, SUB + rows), slice(0, SUB), slice(SUB + rows, total_rows)
    fields = []
    for own, full, factor in ((e_in, fe, None), (h_in, fh, courant), (t_in, ft, courant * courant)):
        fields += [(own, full, factor, c) for c in range(own.shape[0])]
    count = len(fields)

    def scaled_to(factor, value):
        return value if factor is None else value * factor

    for k, (own, full, factor, c) in enumerate(fields):
        for n in range(full.shape[1]):
            full[c, n, top, :] = jnp.zeros((SUB, LANE), jnp.float32)
            full[c, n, bottom, :] = jnp.zeros((SUB, LANE), jnp.float32)
        for begin, side, tail in ((0, low_y, True), (SIDE + width, high_y, False)):
            value = side(from_lanes(ya, k, count, tail), from_lanes(yb, k, count, tail))
            put(full, c, inner, begin, scaled_to(factor, value))
    place_rows(fe, fh, ft, rows, SIDE, lambda s: low_x(xa[s], xb[s]), lambda s: high_x(xa[s], xb[s]))
    for copy in copies:
        copy.wait()
    for own, full, factor, c in fields:
        put(full, c, inner, SIDE, scaled_to(factor, own[c]))


def main_body(fe_in, fh_in, ft_in, s_far, ca, cb, inverse, fe, fh, ft, scaled, to_a, to_b, saved, sems, fg):
    del fe_in, fh_in, ft_in
    (frames,) = fetch((s_far,), (saved,), sems)
    rows, width = scaled.shape
    total_rows = fe.shape[2]
    tiles = total_rows // SUB
    low_x, high_x = sorter("gx")
    low_y, high_y = sorter("gy")
    even_x = is_even("gx")

    height = up_to(FULL * 15 + EXTRA, 2 * SUB)
    for begin, side, tail in ((0, low_y, True), (SIDE + width, high_y, False)):
        packets = [side(a, b) for a, b in zip(from_corners(ca, height, tail), from_corners(cb, height, tail))]
        low, high = low_x(*packets), high_x(*packets)
        place_rows(fe, fh, ft, rows, begin, lambda s, low=low: low[s], lambda s, high=high: high[s])

    inside_x = jnp.where(lax.axis_index("gx") > 0, 1.0, 0.0).astype(jnp.float32)
    inside_y = jnp.where(lax.axis_index("gy") > 0, 1.0, 0.0).astype(jnp.float32)
    lane = lax.broadcasted_iota(jnp.int32, (SUB, LANE), 1)
    depths = [lax.rem(lane + n * LANE, NZ) for n in range(NZ // math.gcd(NZ, LANE))]
    uppers = [(d != NZ - 1).astype(jnp.float32) for d in depths]
    lowers = [(d != 0).astype(jnp.float32) for d in depths]

    sub = lax.broadcasted_iota(jnp.int32, (SUB, LANE), 0)
    joint = tiles - 1
    joint_mask = jnp.where(sub >= SUB // 2, inside_x, 1.0)

    def at(r, shift=0):
        return slice(r * SUB + shift, (r + 1) * SUB + shift)

    def tiles_of(before, after):
        return range((SIDE - before * NZ) // LANE, up_to(SIDE + width + after * NZ, LANE) // LANE)

    def ahead(values, places, n):
        turned = pltpu.roll(values[n], LANE - places, 1)
        if n + 1 not in values or (places == 1 and (n + 1) * LANE % NZ == 0):
            return turned
        return jnp.where(lane < LANE - places, turned, pltpu.roll(values[n + 1], LANE - places, 1))

    def behind(values, places, n):
        turned = pltpu.roll(values[n], places, 1)
        if n - 1 not in values or (places == 1 and n * LANE % NZ == 0):
            return turned
        return jnp.where(lane >= places, turned, pltpu.roll(values[n - 1], places, 1))

    for step in range(STEPS):
        left = STEPS - 1 - step
        lanes_g, lanes_h, lanes_e = tiles_of(left + 1, left + 1), tiles_of(left + 1, left), tiles_of(left, left)
        last = left == 0
        g = [[{}, {}, {}] for _ in range(tiles)]
        h = [[{}, {}, {}] for _ in range(tiles)]
        joined = left + 1 <= SUB // 2
        if joined and left + 2 > SUB // 2:
            for full in (fe, fh, ft):
                for c in range(full.shape[0]):
                    for n in lanes_g:
                        full[c, n, at(joint), :] = jnp.where(
                            sub < SUB // 2, full[c, n, at(joint), :], full[c, n, at(0), :]
                        )

        def turn(r, n):
            e = [fe[c, n, at(r), :] for c in range(3)]
            for c in range(3):
                t = [ft[3 * i + c, n, at(r), :] for i in range(3)]
                g[r][c][n] = (t[0] * e[0] + t[1] * e[1]) + t[2] * e[2]
                if c > 0:
                    fg[c - 1, n, at(r), :] = g[r][c][n]
                    if joined and r == 1:
                        fg[c - 1, n, at(tiles), :] = g[r][c][n]

        def update_h(r, n):
            upper = uppers[n % len(uppers)]
            own = g[r]
            if r == tiles - 1 and not joined:
                next_x = [None] + [pltpu.roll(own[c][n], SUB - 1, 0) for c in (1, 2)]
            else:
                next_x = [None] + [fg[c - 1, n, at(r, 1), :] for c in (1, 2)]
            curl = [
                (ahead(own[2], NZ, n) - own[2][n]) - (ahead(own[1], 1, n) * upper - own[1][n]),
                (ahead(own[0], 1, n) * upper - own[0][n]) - (next_x[2] - own[2][n]),
                (next_x[1] - own[1][n]) - (ahead(own[0], NZ, n) - own[0][n]),
            ]
            for c in range(3):
                value = fh[c, n, at(r), :] - curl[c]
                if r == 0:
                    value = value * inside_x
                if r == joint and joined:
                    value = value * joint_mask
                if n < SIDE // LANE:
                    value = value * inside_y
                fh[c, n, at(r), :] = value
                if r == joint and joined and c > 0:
                    fh[c, n, at(0), :] = value
                h[r][c][n] = value

        def update_e(r, n):
            lower = lowers[n % len(lowers)]
            own = h[r]
            if r == 0:
                prev_x = [None] + [pltpu.roll(own[c][n], 1, 0) for c in (1, 2)]
            else:
                prev_x = [None] + [fh[c, n, at(r, -1), :] for c in (1, 2)]
            curl = [
                (own[2][n] - behind(own[2], NZ, n)) - (own[1][n] - behind(own[1], 1, n) * lower),
                (own[0][n] - behind(own[0], 1, n) * lower) - (own[2][n] - prev_x[2]),
                (own[1][n] - prev_x[1]) - (own[0][n] - behind(own[0], NZ, n)),
            ]
            for c in range(3):
                fe[c, n, at(r), :] = fe[c, n, at(r), :] + curl[c]

        if joined:
            inner = list(range(tiles - 2, 0, -1))
            stages = [(joint, None, None)] + [
                (r, r, r + 1 if n > 0 else None) for n, r in enumerate(inner)
            ]
            stages += [(None, joint, None), (None, None, 1)] + ([] if last else [(None, None, joint)])
        else:
            stages = [(r - 1 if r > 0 else None, r if r < tiles else None, r + 1 if r + 1 < tiles else None) for r in range(tiles, -2, -1)]
            stages = [(a, b if b is not None and b >= 0 else None, c) for a, b, c in stages]
        for to_turn, to_h, to_e in stages:
            for n in lanes_g:
                if to_turn is not None:
                    turn(to_turn, n)
            for n in lanes_g:
                if to_h is not None and n in lanes_h:
                    update_h(to_h, n)
                if to_e is not None and n in lanes_e:
                    update_e(to_e, n)

        if step == 0:
            frames.wait()
        pair = 2 * SUB
        for r in range(rows // pair):
            for n in range(width // LANE):
                here = slice(r * pair, (r + 1) * pair)
                full = slice(SUB + r * pair, SUB + (r + 1) * pair)
                lanes = slice(n * LANE, (n + 1) * LANE)
                s = [saved[step, c, here, lanes].astype(jnp.float32) for c in range(3)]
                e = [fe[c, n + SIDE // LANE, full, :] for c in range(3)]
                term = (e[0] * s[0] + e[1] * s[1]) + e[2] * s[2]
                scaled[here, lanes] = term if step == 0 else scaled[here, lanes] + term

    scaled[...] = scaled[...] * inverse[...]
    head, tail = scaled[:RADIUS], scaled[rows - RADIUS :]
    to_a[...] = jnp.where(even_x, tail, head)
    to_b[...] = jnp.where(even_x, head, tail)


def emit_body(fe, fh, e_out, h_out):
    rows, width = e_out.shape[1:]
    for c in range(3):
        for n in range(width // LANE):
            lanes = slice(n * LANE, (n + 1) * LANE)
            e_out[c, :, lanes] = fe[c, n + SIDE // LANE, SUB : SUB + rows, :]
            h_out[c, :, lanes] = fh[c, n + SIDE // LANE, SUB : SUB + rows, :] * (1.0 / courant)


def box(values, unit, axis):
    size = values.shape[axis]

    def ahead(v, places):
        return pltpu.roll(v, size - places * unit, axis)

    two = values + ahead(values, 1)
    four = two + ahead(two, 2)
    eight = four + ahead(four, 4)
    return eight + ahead(values, 8)


def filter_rows(scaled, xa, xb, across, to_a, to_b):
    rows, width = scaled.shape
    even_y = is_even("gy")
    low, high = sorter("gx")
    a, b = xa[...], xb[...]
    extended = jnp.concatenate([low(a, b), scaled[...], high(a, b)], axis=0)
    result = box(box(extended, 1, 0), 1, 0)[:rows] * (1.0 / (RADIUS + 1.0))
    across[...] = result
    head, tail = result[:, :REACH], result[:, width - REACH :]
    to_a[...] = jnp.where(even_y, tail, head)
    to_b[...] = jnp.where(even_y, head, tail)


def filter_columns(across, ya, yb, gradient):
    width = across.shape[1]
    low, high = sorter("gy")
    for r in range(across.shape[0] // SUB):
        at = slice(r * SUB, (r + 1) * SUB)
        a, b = ya[at], yb[at]
        extended = jnp.concatenate([low(a, b), across[at], high(a, b)], axis=1)
        gradient[at] = box(box(extended, NZ, 1), NZ, 1)[:, :width] * (1.0 / (RADIUS + 1.0))


def tent(offset):
    return (RADIUS + 1.0 - abs(offset)) / (RADIUS + 1.0)


def coverage(places, length):
    total = jnp.zeros(places.shape, jnp.float32)
    for offset in range(-RADIUS, RADIUS + 1):
        inside = ((places + offset >= 0) & (places + offset < length)).astype(jnp.float32)
        total = total + tent(offset) * inside
    return total


def shards(electric, magnetic, tensor, saved):
    rows, width = electric.shape[1:]
    cols = width // NZ
    edge = (RADIUS, width)
    full = ((width + 2 * SIDE) // LANE, rows + 2 * SUB, LANE)
    fulls = [(n, *full) for n in (3, 3, 9)]

    own = (electric, magnetic, tensor)
    xa, xb = swap(*pack_x(electric, magnetic, tensor), "gx", "gy")
    count = electric.shape[0] + magnetic.shape[0] + tensor.shape[0]
    packet = (count + -(-count // (2 * PER_TILE)), rows, WHOLE)
    ya, yb = swap(*call(pack_lanes, [packet, packet], own, room(*own), limit=8, far=(0, 1, 2)), "gy", "gx", fill=False)
    height = xa.shape[0]
    packet = (2 * height + up_to(height // 4, SUB), WHOLE)
    ca, cb = swap(*call(pack_corners, [packet, packet], (xa, xb), limit=8), "gy", "gx")

    row_places = lax.axis_index("gx") * rows + lax.broadcasted_iota(jnp.int32, (rows, width), 0)
    col_places = lax.axis_index("gy") * cols + lax.broadcasted_iota(jnp.int32, (rows, width), 1) // NZ
    cover = coverage(row_places, lax.axis_size("gx") * rows) * coverage(col_places, lax.axis_size("gy") * cols)

    fields = call(assemble_body, fulls, (*own, xa, xb, ya, yb), room(*own), cost=2**22, far=(0, 1, 2))
    fe, fh, _, scaled, to_a, to_b = call(
        main_body,
        [*fulls, (rows, width), edge, edge],
        (*fields, saved, ca, cb, 1.0 / cover),
        [*room(saved), pltpu.VMEM((2, full[0], full[1] + SUB, LANE), jnp.float32)],
        limit=20,
        far=(3,),
        aliases={0: 0, 1: 1, 2: 2},
        cost=2**23,
    )
    xa, xb = swap(to_a, to_b, "gx", "gy")
    e, h = call(emit_body, [electric.shape, magnetic.shape], (fe, fh))
    side = (rows, REACH)
    across, to_a, to_b = call(filter_rows, [(rows, width), side, side], (scaled, xa, xb))
    ya, yb = swap(to_a, to_b, "gy", "gx")
    (gradient,) = call(filter_columns, [(rows, width)], (across, ya, yb))
    return e, h, gradient


def solution(mesh):
    in_specs = (
        P(None, "gx", "gy"),
        P(None, "gx", "gy"),
        P(None, "gx", "gy"),
        P(None, None, "gx", "gy"),
    )
    out_specs = (P(None, "gx", "gy"), P(None, "gx", "gy"), P("gx", "gy"))
    return jax.shard_map(shards, mesh=mesh, in_specs=in_specs, out_specs=out_specs, check_vma=False)
```

```python
import math

import jax
import jax.numpy as jnp
from jax import lax
from jax.experimental import pallas as pl
from jax.experimental.pallas import tpu as pltpu
from jax.sharding import PartitionSpec as P


NZ = 48
STEPS = 6
RADIUS = 8
SUB = 8
LANE = 128

courant = 0.45


def up_to(size, unit):
    return -(-size // unit) * unit


HALO = STEPS
SIDE = up_to(HALO * NZ, LANE)
WHOLE = HALO * NZ // LANE * LANE
REST = HALO * NZ - WHOLE
PER_TILE = LANE // REST
REACH = RADIUS * NZ
AXES = ("gx", "gy")
PACK_LIMIT = 8


def neighbours(axis, other, first, fill, apart=False):
    count, wide = lax.axis_size(axis), lax.axis_size(other)
    pairs = [((i, j), (i + 1, j)) for i in range(first, count - 1, 2) for j in range(wide)]
    if fill and wide % 2 == 0:
        paired = {i for i, _ in (p for pair in pairs for p in pair)}
        idle = [i for i in range(count) if i not in paired]
        step = wide // 2 if apart else 1
        pairs += [((i, j), (i, j + step)) for i in idle for j in range(wide) if j // step % 2 == 0]
    route = []
    for (i, j), (k, m) in pairs:
        one, two = (i * wide + j, k * wide + m) if axis == AXES[0] else (j * count + i, m * count + k)
        route += [(one, two), (two, one)]
    return route


def swap(to_a, to_b, axis, other, fill=True, apart=False):
    from_b = lax.ppermute(to_b, AXES, neighbours(axis, other, 1, fill, apart))
    from_a = lax.ppermute(to_a, AXES, neighbours(axis, other, 0, fill))
    return from_a, from_b


def is_even(axis):
    return lax.rem(lax.axis_index(axis), 2) == 0


def sorter(axis):
    index = lax.axis_index(axis)
    even = lax.rem(index, 2) == 0
    starts, ends = index == 0, index == lax.axis_size(axis) - 1

    def low(a, b):
        return jnp.where(starts, 0.0, jnp.where(even, b, a))

    def high(a, b):
        return jnp.where(ends, 0.0, jnp.where(even, a, b))

    return low, high


def call(body, outs, ins, scratch=(), limit=16, aliases=None, cost=2**20, far=()):
    vmem = pl.BlockSpec(memory_space=pltpu.VMEM)
    hbm = pl.BlockSpec(memory_space=pltpu.HBM)
    specs = [hbm if n in far else vmem for n in range(len(ins))]
    ins = [pltpu.with_memory_space_constraint(x, pltpu.HBM) if n in far else x for n, x in enumerate(ins)]
    return pl.pallas_call(
        body,
        out_shape=[jax.ShapeDtypeStruct(s, jnp.float32) if isinstance(s, tuple) else s for s in outs],
        in_specs=specs,
        out_specs=[vmem] * len(outs),
        scratch_shapes=list(scratch),
        input_output_aliases=aliases or {},
        cost_estimate=pl.CostEstimate(flops=cost, bytes_accessed=cost, transcendentals=0),
        compiler_params=pltpu.CompilerParams(vmem_limit_bytes=limit * 2**20),
    )(*ins)


FULL = HALO - 1
EXTRA = 3


def columns_of(t, e, row):
    rows = slice(row, row + 1)
    return [
        (t[c, rows] * e[0, rows] + t[3 + c, rows] * e[1, rows]) + t[6 + c, rows] * e[2, rows] for c in range(3)
    ]


def pack_rows(e_hbm, h_hbm, t_hbm, to_a, to_b, e_rows, h_rows, t_rows, sems):
    rows = e_hbm.shape[1]
    copies = []
    for n, (source, target) in enumerate(((e_hbm, e_rows), (h_hbm, h_rows), (t_hbm, t_rows))):
        for side, begin in enumerate((0, rows - SUB)):
            copies.append(
                pltpu.make_async_copy(source.at[:, begin : begin + SUB, :], target.at[side], sems.at[n, side])
            )
            copies[-1].start()
    for copy in copies:
        copy.wait()
    even = is_even("gx")
    at = 0

    def put(head, tail):
        nonlocal at
        size = head.shape[0]
        to_a[at : at + size, :] = jnp.where(even, tail, head)
        to_b[at : at + size, :] = jnp.where(even, head, tail)
        at += size

    for part in (e_rows, h_rows, t_rows):
        for c in range(part.shape[1]):
            put(part[0, c, 0:FULL, :], part[1, c, SUB - FULL : SUB, :])
    ahead = columns_of(t_rows.at[0], e_rows.at[0], FULL)
    row = SUB - HALO
    g = columns_of(t_rows.at[1], e_rows.at[1], row)
    put(ahead[1], g[0])
    put(ahead[2], h_rows[1, 1, row : row + 1] - courant * g[2])
    put(jnp.zeros_like(g[0]), h_rows[1, 2, row : row + 1] + courant * g[1])
    spare = to_a.shape[0] - at
    nothing = jnp.zeros((spare, to_a.shape[1]), jnp.float32)
    put(nothing, nothing)


def pack_x(electric, magnetic, tensor):
    width = electric.shape[2]
    parts = (electric, magnetic, tensor)
    packed = up_to(FULL * sum(part.shape[0] for part in parts) + EXTRA, 2 * SUB)
    out = jax.ShapeDtypeStruct((packed, width), jnp.float32)
    return pl.pallas_call(
        pack_rows,
        name="pack_x",
        out_shape=[out, out],
        in_specs=[pl.BlockSpec(memory_space=pltpu.HBM)] * 3,
        out_specs=[pl.BlockSpec(memory_space=pltpu.VMEM)] * 2,
        scratch_shapes=[pltpu.VMEM((2, part.shape[0], SUB, width), jnp.float32) for part in parts]
        + [pltpu.SemaphoreType.DMA((3, 2))],
        compiler_params=pltpu.CompilerParams(vmem_limit_bytes=PACK_LIMIT * 2**20),
    )(*(pltpu.with_memory_space_constraint(part, pltpu.HBM) for part in parts))


def fetch(sources, targets, sems):
    copies = [pltpu.make_async_copy(s, t, sems.at[n]) for n, (s, t) in enumerate(zip(sources, targets))]
    for copy in copies:
        copy.start()
    return copies


def room(*arrays):
    return [pltpu.VMEM(x.shape, x.dtype) for x in arrays] + [pltpu.SemaphoreType.DMA((len(arrays),))]


def quarters(parts):
    slot = lax.broadcasted_iota(jnp.int32, parts[0][0].shape, 1) // REST
    result = None
    for n, (part, first) in enumerate(parts):
        turn = (n * REST - first) % LANE
        turned = pltpu.roll(part, turn, 1) if turn else part
        result = turned if result is None else jnp.where(slot == n, turned, result)
    return result


def whole_and_rest(width, tail):
    if tail:
        return width - WHOLE, width - WHOLE - LANE, LANE - REST
    return 0, WHOLE, 0


def pack_lanes(e_far, h_far, t_far, to_a, to_b, e_in, h_in, t_in, sems):
    for copy in fetch((e_far, h_far, t_far), (e_in, h_in, t_in), sems):
        copy.wait()
    even = is_even("gy")
    width = e_in.shape[2]
    fields = [ref.at[c] for ref in (e_in, h_in, t_in) for c in range(ref.shape[0])]
    made = []
    for tail in (False, True):
        whole, rest, first = whole_and_rest(width, tail)
        blocks = [f[:, whole : whole + WHOLE] for f in fields]
        for n in range(0, len(fields), PER_TILE):
            blocks.append(quarters([(f[:, rest : rest + LANE], first) for f in fields[n : n + PER_TILE]]))
        made.append(blocks)
    count = len(fields)
    for k, (head, tail) in enumerate(zip(*made)):
        if k < count:
            at, lanes = k, slice(0, WHOLE)
        else:
            at, half = count + (k - count) // 2, (k - count) % 2
            lanes = slice(half * LANE, (half + 1) * LANE)
        to_a[at, :, lanes] = jnp.where(even, tail, head)
        to_b[at, :, lanes] = jnp.where(even, head, tail)


def from_lanes(ref, k, count, tail):
    group, slot = k // PER_TILE, k % PER_TILE
    at, half = count + group // 2, group % 2
    first = LANE - REST if tail else 0
    turn = (first - slot * REST) % LANE
    rest = ref[at, :, half * LANE : (half + 1) * LANE]
    rest = pltpu.roll(rest, turn, 1) if turn else rest
    whole = ref[k]
    return jnp.concatenate([rest, whole] if tail else [whole, rest], axis=1)


def pack_corners(xa, xb, to_a, to_b):
    even = is_even("gy")
    height, width = xa.shape
    half = height // 2
    made = []
    for tail in (False, True):
        whole, rest, first = whole_and_rest(width, tail)
        pieces = [
            (x[at : at + half, rest : rest + LANE], first) for x in (xa, xb) for at in (0, half)
        ]
        made.append((xa[:, whole : whole + WHOLE], xb[:, whole : whole + WHOLE], quarters(pieces)))
    upper = up_to(half // 2, SUB)
    for out, (blocks_even, blocks_odd) in ((to_a, (made[1], made[0])), (to_b, (made[0], made[1]))):
        one, two, rest = (jnp.where(even, p, q) for p, q in zip(blocks_even, blocks_odd))
        out[0:height] = one
        out[height : 2 * height] = two
        out[2 * height : 2 * height + upper, 0:LANE] = rest[:upper]
        out[2 * height : 2 * height + half - upper, LANE:] = rest[upper:]
        if 2 * upper > half:
            out[2 * height + half - upper :, LANE:] = jnp.zeros((2 * upper - half, LANE), jnp.float32)


def from_corners(ref, height, tail):
    half = height // 2
    upper = up_to(half // 2, SUB)
    base = 2 * height
    rest = jnp.concatenate([ref[base : base + upper, 0:LANE], ref[base : base + half - upper, LANE:]], axis=0)
    first = LANE - REST if tail else 0
    result = []
    for n in range(2):
        turned = []
        for m in range(2):
            turn = (first - (2 * n + m) * REST) % LANE
            turned.append(pltpu.roll(rest, turn, 1) if turn else rest)
        rest_n = jnp.concatenate(turned, axis=0)
        whole = ref[n * height : (n + 1) * height]
        result.append(jnp.concatenate([rest_n, whole] if tail else [whole, rest_n], axis=1))
    return result


def put(full, c, rows, begin, value):
    for n in range(value.shape[1] // LANE):
        full[c, begin // LANE + n, rows, :] = value[:, n * LANE : (n + 1) * LANE]


def place_rows(full_e, full_h, full_t, rows, begin, low, high):
    fields = [(full_e, c, None) for c in range(3)] + [(full_h, c, courant) for c in range(3)]
    fields += [(full_t, c, courant * courant) for c in range(9)]
    top, bottom = slice(SUB - FULL, SUB), slice(SUB + rows, SUB + rows + FULL)
    for k, (full, c, factor) in enumerate(fields):
        packet = slice(k * FULL, (k + 1) * FULL)
        for at, get in ((top, low), (bottom, high)):
            value = get(packet)
            put(full, c, at, begin, value if factor is None else value * factor)
    base = len(fields) * FULL
    extra = [slice(base + i, base + i + 1) for i in range(EXTRA)]
    top, bottom = slice(SUB - HALO, SUB - FULL), slice(SUB + rows + FULL, SUB + rows + HALO)
    put(full_t, 0, top, begin, low(extra[0]) * (courant * courant))
    put(full_h, 1, top, begin, low(extra[1]) * courant)
    put(full_h, 2, top, begin, low(extra[2]) * courant)
    put(full_t, 1, bottom, begin, high(extra[0]) * (courant * courant))
    put(full_t, 2, bottom, begin, high(extra[1]) * (courant * courant))
    one = jnp.ones_like(low(extra[0]))
    put(full_e, 0, top, begin, one)
    put(full_e, 0, bottom, begin, one)


def sweeper(fe, fh, ft, fg, width):
    tiles = fe.shape[2] // SUB
    inside_x = jnp.where(lax.axis_index("gx") > 0, 1.0, 0.0).astype(jnp.float32)
    inside_y = jnp.where(lax.axis_index("gy") > 0, 1.0, 0.0).astype(jnp.float32)
    lane = lax.broadcasted_iota(jnp.int32, (SUB, LANE), 1)
    depths = [lax.rem(lane + n * LANE, NZ) for n in range(NZ // math.gcd(NZ, LANE))]
    uppers = [(d != NZ - 1).astype(jnp.float32) for d in depths]
    lowers = [(d != 0).astype(jnp.float32) for d in depths]

    sub = lax.broadcasted_iota(jnp.int32, (SUB, LANE), 0)
    joint = tiles - 1
    joint_mask = jnp.where(sub >= SUB // 2, inside_x, 1.0)

    def at(r, shift=0):
        return slice(r * SUB + shift, (r + 1) * SUB + shift)

    def tiles_of(before, after):
        return range((SIDE - before * NZ) // LANE, up_to(SIDE + width + after * NZ, LANE) // LANE)

    def ahead(values, places, n):
        turned = pltpu.roll(values[n], LANE - places, 1)
        if n + 1 not in values or (places == 1 and (n + 1) * LANE % NZ == 0):
            return turned
        return jnp.where(lane < LANE - places, turned, pltpu.roll(values[n + 1], LANE - places, 1))

    def behind(values, places, n):
        turned = pltpu.roll(values[n], places, 1)
        if n - 1 not in values or (places == 1 and n * LANE % NZ == 0):
            return turned
        return jnp.where(lane >= places, turned, pltpu.roll(values[n - 1], places, 1))

    def sweep(step, part):
        left = STEPS - 1 - step
        lanes_g, lanes_h, lanes_e = tiles_of(left + 1, left + 1), tiles_of(left + 1, left), tiles_of(left, left)
        last = left == 0
        g = [[{}, {}, {}] for _ in range(tiles)]
        h = [[{}, {}, {}] for _ in range(tiles)]
        joined = left + 1 <= SUB // 2
        if joined and left + 2 > SUB // 2:
            for full in (fe, fh, ft):
                for c in range(full.shape[0]):
                    for n in lanes_g:
                        full[c, n, at(joint), :] = jnp.where(
                            sub < SUB // 2, full[c, n, at(joint), :], full[c, n, at(0), :]
                        )

        def turn(r, n):
            e = [fe[c, n, at(r), :] for c in range(3)]
            for c in range(3):
                t = [ft[3 * i + c, n, at(r), :] for i in range(3)]
                g[r][c][n] = (t[0] * e[0] + t[1] * e[1]) + t[2] * e[2]
                if c > 0:
                    fg[c - 1, n, at(r), :] = g[r][c][n]
                    if joined and r == 1:
                        fg[c - 1, n, at(tiles), :] = g[r][c][n]

        def update_h(r, n):
            upper = uppers[n % len(uppers)]
            own = g[r]
            if r == tiles - 1 and not joined:
                next_x = [None] + [pltpu.roll(own[c][n], SUB - 1, 0) for c in (1, 2)]
            else:
                next_x = [None] + [fg[c - 1, n, at(r, 1), :] for c in (1, 2)]
            curl = [
                (ahead(own[2], NZ, n) - own[2][n]) - (ahead(own[1], 1, n) * upper - own[1][n]),
                (ahead(own[0], 1, n) * upper - own[0][n]) - (next_x[2] - own[2][n]),
                (next_x[1] - own[1][n]) - (ahead(own[0], NZ, n) - own[0][n]),
            ]
            for c in range(3):
                value = fh[c, n, at(r), :] - curl[c]
                if r == 0:
                    value = value * inside_x
                if r == joint and joined:
                    value = value * joint_mask
                if n < SIDE // LANE:
                    value = value * inside_y
                fh[c, n, at(r), :] = value
                if r == joint and joined and c > 0:
                    fh[c, n, at(0), :] = value
                h[r][c][n] = value

        def update_e(r, n):
            lower = lowers[n % len(lowers)]
            own = h[r]
            if r == 0:
                prev_x = [None] + [pltpu.roll(own[c][n], 1, 0) for c in (1, 2)]
            else:
                prev_x = [None] + [fh[c, n, at(r, -1), :] for c in (1, 2)]
            curl = [
                (own[2][n] - behind(own[2], NZ, n)) - (own[1][n] - behind(own[1], 1, n) * lower),
                (own[0][n] - behind(own[0], 1, n) * lower) - (own[2][n] - prev_x[2]),
                (own[1][n] - prev_x[1]) - (own[0][n] - behind(own[0], NZ, n)),
            ]
            for c in range(3):
                fe[c, n, at(r), :] = fe[c, n, at(r), :] + curl[c]

        inner = list(range(tiles - 2, 0, -1))
        if joined:
            stages = [(joint, None, None)] + [
                (r, r, r + 1 if n > 0 else None) for n, r in enumerate(inner)
            ]
            stages += [(None, joint, None), (None, None, 1)] + ([] if last else [(None, None, joint)])
        elif part == "inner":
            stages = [(inner[0], None, None)] + [
                (r, r, r + 1 if n > 0 else None) for n, r in enumerate(inner[1:])
            ]
        elif part == "rest":
            stages = [(joint, None, None), (joint - 1, joint, None), (None, joint - 1, joint), (1, None, joint - 1)]
            stages += [(0, None, None), (None, 0, 1), (None, None, 0)]
            h[1] = [{n: fh[c, n, at(1), :] for n in lanes_h} for c in range(3)]
        else:
            stages = [(r - 1, r, r + 1) for r in range(tiles, -2, -1)]
            stages = [[r if 0 <= r < tiles else None for r in stage] for stage in stages]
        for to_turn, to_h, to_e in stages:
            for n in lanes_g:
                if to_turn is not None:
                    turn(to_turn, n)
            for n in lanes_g:
                if to_h is not None and n in lanes_h:
                    update_h(to_h, n)
                if to_e is not None and n in lanes_e:
                    update_e(to_e, n)

    return sweep


def assemble_body(e_far, h_far, t_far, s_far, xa, xb, ya, yb, fe, fh, ft, saved, e_in, h_in, t_in, sems, fg):
    *copies, frames = fetch((e_far, h_far, t_far, s_far), (e_in, h_in, t_in, saved), sems)
    rows, width = e_in.shape[1:]
    total_rows = fe.shape[2]
    low_x, high_x = sorter("gx")
    low_y, high_y = sorter("gy")
    inner, top, bottom = slice(SUB, SUB + rows), slice(0, SUB), slice(SUB + rows, total_rows)
    fields = []
    for own, full, factor in ((e_in, fe, None), (h_in, fh, courant), (t_in, ft, courant * courant)):
        fields += [(own, full, factor, c) for c in range(own.shape[0])]
    count = len(fields)

    def scaled_to(factor, value):
        return value if factor is None else value * factor

    for k, (own, full, factor, c) in enumerate(fields):
        for n in range(full.shape[1]):
            full[c, n, top, :] = jnp.zeros((SUB, LANE), jnp.float32)
            full[c, n, bottom, :] = jnp.zeros((SUB, LANE), jnp.float32)
        for begin, side, tail in ((0, low_y, True), (SIDE + width, high_y, False)):
            value = side(from_lanes(ya, k, count, tail), from_lanes(yb, k, count, tail))
            put(full, c, inner, begin, scaled_to(factor, value))
    place_rows(fe, fh, ft, rows, SIDE, lambda s: low_x(xa[s], xb[s]), lambda s: high_x(xa[s], xb[s]))
    for copy in copies:
        copy.wait()
    for own, full, factor, c in fields:
        put(full, c, inner, SIDE, scaled_to(factor, own[c]))
    sweeper(fe, fh, ft, fg, width)(0, "inner")
    frames.wait()


def main_body(fe_in, fh_in, ft_in, saved, ca, cb, inverse, fe, fh, ft, scaled, to_a, to_b, fg):
    del fe_in, fh_in, ft_in
    rows, width = scaled.shape
    low_x, high_x = sorter("gx")
    low_y, high_y = sorter("gy")
    even_x = is_even("gx")

    height = up_to(FULL * 15 + EXTRA, 2 * SUB)
    for begin, side, tail in ((0, low_y, True), (SIDE + width, high_y, False)):
        packets = [side(a, b) for a, b in zip(from_corners(ca, height, tail), from_corners(cb, height, tail))]
        low, high = low_x(*packets), high_x(*packets)
        place_rows(fe, fh, ft, rows, begin, lambda s, low=low: low[s], lambda s, high=high: high[s])

    sweep = sweeper(fe, fh, ft, fg, width)
    for step in range(STEPS):
        sweep(step, "rest" if step == 0 else "all")
        pair = 2 * SUB
        for r in range(rows // pair):
            for n in range(width // LANE):
                here = slice(r * pair, (r + 1) * pair)
                full = slice(SUB + r * pair, SUB + (r + 1) * pair)
                lanes = slice(n * LANE, (n + 1) * LANE)
                s = [saved[step, c, here, lanes].astype(jnp.float32) for c in range(3)]
                e = [fe[c, n + SIDE // LANE, full, :] for c in range(3)]
                term = (e[0] * s[0] + e[1] * s[1]) + e[2] * s[2]
                scaled[here, lanes] = term if step == 0 else scaled[here, lanes] + term

    scaled[...] = scaled[...] * inverse[...]
    head, tail = scaled[:RADIUS], scaled[rows - RADIUS :]
    to_a[...] = jnp.where(even_x, tail, head)
    to_b[...] = jnp.where(even_x, head, tail)


def emit_body(fe, fh, e_out, h_out):
    rows, width = e_out.shape[1:]
    for c in range(3):
        for n in range(width // LANE):
            lanes = slice(n * LANE, (n + 1) * LANE)
            e_out[c, :, lanes] = fe[c, n + SIDE // LANE, SUB : SUB + rows, :]
            h_out[c, :, lanes] = fh[c, n + SIDE // LANE, SUB : SUB + rows, :] * (1.0 / courant)


def box(values, unit, axis):
    size = values.shape[axis]

    def ahead(v, places):
        return pltpu.roll(v, size - places * unit, axis)

    two = values + ahead(values, 1)
    four = two + ahead(two, 2)
    eight = four + ahead(four, 4)
    return eight + ahead(values, 8)


def filter_rows(scaled, xa, xb, across, to_a, to_b):
    rows, width = scaled.shape
    even_y = is_even("gy")
    low, high = sorter("gx")
    a, b = xa[...], xb[...]
    extended = jnp.concatenate([low(a, b), scaled[...], high(a, b)], axis=0)
    result = box(box(extended, 1, 0), 1, 0)[:rows] * (1.0 / (RADIUS + 1.0))
    across[...] = result
    head, tail = result[:, :REACH], result[:, width - REACH :]
    to_a[...] = jnp.where(even_y, tail, head)
    to_b[...] = jnp.where(even_y, head, tail)


def filter_columns(across, ya, yb, gradient):
    width = across.shape[1]
    low, high = sorter("gy")
    for r in range(across.shape[0] // SUB):
        at = slice(r * SUB, (r + 1) * SUB)
        a, b = ya[at], yb[at]
        extended = jnp.concatenate([low(a, b), across[at], high(a, b)], axis=1)
        gradient[at] = box(box(extended, NZ, 1), NZ, 1)[:, :width] * (1.0 / (RADIUS + 1.0))


def tent(offset):
    return (RADIUS + 1.0 - abs(offset)) / (RADIUS + 1.0)


def coverage(places, length):
    total = jnp.zeros(places.shape, jnp.float32)
    for offset in range(-RADIUS, RADIUS + 1):
        inside = ((places + offset >= 0) & (places + offset < length)).astype(jnp.float32)
        total = total + tent(offset) * inside
    return total


def shards(electric, magnetic, tensor, saved):
    rows, width = electric.shape[1:]
    cols = width // NZ
    edge = (RADIUS, width)
    full = ((width + 2 * SIDE) // LANE, rows + 2 * SUB, LANE)
    fulls = [(n, *full) for n in (3, 3, 9)]

    own = (electric, magnetic, tensor)
    xa, xb = swap(*pack_x(electric, magnetic, tensor), "gx", "gy")
    count = electric.shape[0] + magnetic.shape[0] + tensor.shape[0]
    packet = (count + -(-count // (2 * PER_TILE)), rows, WHOLE)
    ya, yb = swap(*call(pack_lanes, [packet, packet], own, room(*own), limit=8, far=(0, 1, 2)), "gy", "gx", fill=False)
    height = xa.shape[0]
    packet = (2 * height + up_to(height // 4, SUB), WHOLE)
    ca, cb = swap(*call(pack_corners, [packet, packet], (xa, xb), limit=8), "gy", "gx", apart=True)

    row_places = lax.axis_index("gx") * rows + lax.broadcasted_iota(jnp.int32, (rows, width), 0)
    col_places = lax.axis_index("gy") * cols + lax.broadcasted_iota(jnp.int32, (rows, width), 1) // NZ
    cover = coverage(row_places, lax.axis_size("gx") * rows) * coverage(col_places, lax.axis_size("gy") * cols)

    shifted = pltpu.VMEM((2, full[0], full[1] + SUB, LANE), jnp.float32)
    *fields, frames = call(
        assemble_body,
        [*fulls, jax.ShapeDtypeStruct(saved.shape, saved.dtype)],
        (*own, saved, xa, xb, ya, yb),
        [*room(*own)[:-1], pltpu.SemaphoreType.DMA((4,)), shifted],
        cost=2**22,
        far=(0, 1, 2, 3),
    )
    fe, fh, _, scaled, to_a, to_b = call(
        main_body,
        [*fulls, (rows, width), edge, edge],
        (*fields, frames, ca, cb, 1.0 / cover),
        [shifted],
        limit=20,
        aliases={0: 0, 1: 1, 2: 2},
        cost=2**23,
    )
    xa, xb = swap(to_a, to_b, "gx", "gy")
    e, h = call(emit_body, [electric.shape, magnetic.shape], (fe, fh))
    side = (rows, REACH)
    across, to_a, to_b = call(filter_rows, [(rows, width), side, side], (scaled, xa, xb))
    ya, yb = swap(to_a, to_b, "gy", "gx", apart=True)
    (gradient,) = call(filter_columns, [(rows, width)], (across, ya, yb))
    return e, h, gradient


def solution(mesh):
    in_specs = (
        P(None, "gx", "gy"),
        P(None, "gx", "gy"),
        P(None, "gx", "gy"),
        P(None, None, "gx", "gy"),
    )
    out_specs = (P(None, "gx", "gy"), P(None, "gx", "gy"), P("gx", "gy"))
    return jax.shard_map(shards, mesh=mesh, in_specs=in_specs, out_specs=out_specs, check_vma=False)
```

```python
import math

import jax
import jax.numpy as jnp
from jax import lax
from jax.experimental import pallas as pl
from jax.experimental.pallas import tpu as pltpu
from jax.sharding import PartitionSpec as P


NZ = 48
STEPS = 6
RADIUS = 8
SUB = 8
LANE = 128

courant = 0.45


def up_to(size, unit):
    return -(-size // unit) * unit


HALO = STEPS
SIDE = up_to(HALO * NZ, LANE)
WHOLE = HALO * NZ // LANE * LANE
REST = HALO * NZ - WHOLE
PER_TILE = LANE // REST
REACH = RADIUS * NZ
AXES = ("gx", "gy")
PACK_LIMIT = 8


def neighbours(axis, other, first, fill, apart=False):
    count, wide = lax.axis_size(axis), lax.axis_size(other)
    pairs = [((i, j), (i + 1, j)) for i in range(first, count - 1, 2) for j in range(wide)]
    if fill and wide % 2 == 0:
        paired = {i for i, _ in (p for pair in pairs for p in pair)}
        idle = [i for i in range(count) if i not in paired]
        step = wide // 2 if apart else 1
        pairs += [((i, j), (i, j + step)) for i in idle for j in range(wide) if j // step % 2 == 0]
    route = []
    for (i, j), (k, m) in pairs:
        one, two = (i * wide + j, k * wide + m) if axis == AXES[0] else (j * count + i, m * count + k)
        route += [(one, two), (two, one)]
    return route


def swap(to_a, to_b, axis, other, fill=True, apart=False):
    from_b = lax.ppermute(to_b, AXES, neighbours(axis, other, 1, fill, apart))
    from_a = lax.ppermute(to_a, AXES, neighbours(axis, other, 0, fill))
    return from_a, from_b


def is_even(axis):
    return lax.rem(lax.axis_index(axis), 2) == 0


def sorter(axis):
    index = lax.axis_index(axis)
    even = lax.rem(index, 2) == 0
    starts, ends = index == 0, index == lax.axis_size(axis) - 1

    def low(a, b):
        return jnp.where(starts, 0.0, jnp.where(even, b, a))

    def high(a, b):
        return jnp.where(ends, 0.0, jnp.where(even, a, b))

    return low, high


def call(body, outs, ins, scratch=(), limit=16, aliases=None, cost=2**20, far=(), space=pltpu.VMEM):
    vmem = pl.BlockSpec(memory_space=pltpu.VMEM)
    hbm = pl.BlockSpec(memory_space=pltpu.HBM)
    specs = [hbm if n in far else vmem for n in range(len(ins))]
    ins = [pltpu.with_memory_space_constraint(x, pltpu.HBM) if n in far else x for n, x in enumerate(ins)]
    return pl.pallas_call(
        body,
        out_shape=[jax.ShapeDtypeStruct(s, jnp.float32) if isinstance(s, tuple) else s for s in outs],
        in_specs=specs,
        out_specs=[pl.BlockSpec(memory_space=space)] * len(outs),
        scratch_shapes=list(scratch),
        input_output_aliases=aliases or {},
        cost_estimate=pl.CostEstimate(flops=cost, bytes_accessed=cost, transcendentals=0),
        compiler_params=pltpu.CompilerParams(vmem_limit_bytes=limit * 2**20),
    )(*ins)


FULL = HALO - 1
EXTRA = 3


def columns_of(t, e, row):
    rows = slice(row, row + 1)
    return [
        (t[c, rows] * e[0, rows] + t[3 + c, rows] * e[1, rows]) + t[6 + c, rows] * e[2, rows] for c in range(3)
    ]


def pack_rows(e_hbm, h_hbm, t_hbm, to_a, to_b, e_rows, h_rows, t_rows, sems):
    rows = e_hbm.shape[1]
    copies = []
    for n, (source, target) in enumerate(((e_hbm, e_rows), (h_hbm, h_rows), (t_hbm, t_rows))):
        for side, begin in enumerate((0, rows - SUB)):
            copies.append(
                pltpu.make_async_copy(source.at[:, begin : begin + SUB, :], target.at[side], sems.at[n, side])
            )
            copies[-1].start()
    for copy in copies:
        copy.wait()
    even = is_even("gx")
    at = 0

    def put(head, tail):
        nonlocal at
        size = head.shape[0]
        to_a[at : at + size, :] = jnp.where(even, tail, head)
        to_b[at : at + size, :] = jnp.where(even, head, tail)
        at += size

    for part in (e_rows, h_rows, t_rows):
        for c in range(part.shape[1]):
            put(part[0, c, 0:FULL, :], part[1, c, SUB - FULL : SUB, :])
    ahead = columns_of(t_rows.at[0], e_rows.at[0], FULL)
    row = SUB - HALO
    g = columns_of(t_rows.at[1], e_rows.at[1], row)
    put(ahead[1], g[0])
    put(ahead[2], h_rows[1, 1, row : row + 1] - courant * g[2])
    put(jnp.zeros_like(g[0]), h_rows[1, 2, row : row + 1] + courant * g[1])
    spare = to_a.shape[0] - at
    nothing = jnp.zeros((spare, to_a.shape[1]), jnp.float32)
    put(nothing, nothing)


def pack_x(electric, magnetic, tensor):
    width = electric.shape[2]
    parts = (electric, magnetic, tensor)
    packed = up_to(FULL * sum(part.shape[0] for part in parts) + EXTRA, 2 * SUB)
    out = jax.ShapeDtypeStruct((packed, width), jnp.float32)
    return pl.pallas_call(
        pack_rows,
        name="pack_x",
        out_shape=[out, out],
        in_specs=[pl.BlockSpec(memory_space=pltpu.HBM)] * 3,
        out_specs=[pl.BlockSpec(memory_space=pltpu.VMEM)] * 2,
        scratch_shapes=[pltpu.VMEM((2, part.shape[0], SUB, width), jnp.float32) for part in parts]
        + [pltpu.SemaphoreType.DMA((3, 2))],
        compiler_params=pltpu.CompilerParams(vmem_limit_bytes=PACK_LIMIT * 2**20),
    )(*(pltpu.with_memory_space_constraint(part, pltpu.HBM) for part in parts))


def fetch(sources, targets, sems):
    copies = [pltpu.make_async_copy(s, t, sems.at[n]) for n, (s, t) in enumerate(zip(sources, targets))]
    for copy in copies:
        copy.start()
    return copies


def room(*arrays):
    return [pltpu.VMEM(x.shape, x.dtype) for x in arrays] + [pltpu.SemaphoreType.DMA((len(arrays),))]


def quarters(parts):
    slot = lax.broadcasted_iota(jnp.int32, parts[0][0].shape, 1) // REST
    result = None
    for n, (part, first) in enumerate(parts):
        turn = (n * REST - first) % LANE
        turned = pltpu.roll(part, turn, 1) if turn else part
        result = turned if result is None else jnp.where(slot == n, turned, result)
    return result


def whole_and_rest(width, tail):
    if tail:
        return width - WHOLE, width - WHOLE - LANE, LANE - REST
    return 0, WHOLE, 0


def pack_lanes(e_far, h_far, t_far, to_a, to_b, e_in, h_in, t_in, sems):
    for copy in fetch((e_far, h_far, t_far), (e_in, h_in, t_in), sems):
        copy.wait()
    even = is_even("gy")
    width = e_in.shape[2]
    fields = [ref.at[c] for ref in (e_in, h_in, t_in) for c in range(ref.shape[0])]
    made = []
    for tail in (False, True):
        whole, rest, first = whole_and_rest(width, tail)
        blocks = [f[:, whole : whole + WHOLE] for f in fields]
        for n in range(0, len(fields), PER_TILE):
            blocks.append(quarters([(f[:, rest : rest + LANE], first) for f in fields[n : n + PER_TILE]]))
        made.append(blocks)
    count = len(fields)
    for k, (head, tail) in enumerate(zip(*made)):
        if k < count:
            at, lanes = k, slice(0, WHOLE)
        else:
            at, half = count + (k - count) // 2, (k - count) % 2
            lanes = slice(half * LANE, (half + 1) * LANE)
        to_a[at, :, lanes] = jnp.where(even, tail, head)
        to_b[at, :, lanes] = jnp.where(even, head, tail)


def from_lanes(ref, k, count, tail):
    group, slot = k // PER_TILE, k % PER_TILE
    at, half = count + group // 2, group % 2
    first = LANE - REST if tail else 0
    turn = (first - slot * REST) % LANE
    rest = ref[at, :, half * LANE : (half + 1) * LANE]
    rest = pltpu.roll(rest, turn, 1) if turn else rest
    whole = ref[k]
    return jnp.concatenate([rest, whole] if tail else [whole, rest], axis=1)


def pack_corners(xa, xb, to_a, to_b):
    even = is_even("gy")
    height, width = xa.shape
    half = height // 2
    made = []
    for tail in (False, True):
        whole, rest, first = whole_and_rest(width, tail)
        pieces = [
            (x[at : at + half, rest : rest + LANE], first) for x in (xa, xb) for at in (0, half)
        ]
        made.append((xa[:, whole : whole + WHOLE], xb[:, whole : whole + WHOLE], quarters(pieces)))
    upper = up_to(half // 2, SUB)
    for out, (blocks_even, blocks_odd) in ((to_a, (made[1], made[0])), (to_b, (made[0], made[1]))):
        one, two, rest = (jnp.where(even, p, q) for p, q in zip(blocks_even, blocks_odd))
        out[0:height] = one
        out[height : 2 * height] = two
        out[2 * height : 2 * height + upper, 0:LANE] = rest[:upper]
        out[2 * height : 2 * height + half - upper, LANE:] = rest[upper:]
        if 2 * upper > half:
            out[2 * height + half - upper :, LANE:] = jnp.zeros((2 * upper - half, LANE), jnp.float32)


def from_corners(ref, height, tail):
    half = height // 2
    upper = up_to(half // 2, SUB)
    base = 2 * height
    rest = jnp.concatenate([ref[base : base + upper, 0:LANE], ref[base : base + half - upper, LANE:]], axis=0)
    first = LANE - REST if tail else 0
    result = []
    for n in range(2):
        turned = []
        for m in range(2):
            turn = (first - (2 * n + m) * REST) % LANE
            turned.append(pltpu.roll(rest, turn, 1) if turn else rest)
        rest_n = jnp.concatenate(turned, axis=0)
        whole = ref[n * height : (n + 1) * height]
        result.append(jnp.concatenate([rest_n, whole] if tail else [whole, rest_n], axis=1))
    return result


def put(full, c, rows, begin, value):
    for n in range(value.shape[1] // LANE):
        full[c, begin // LANE + n, rows, :] = value[:, n * LANE : (n + 1) * LANE]


def place_rows(full_e, full_h, full_t, rows, begin, low, high):
    fields = [(full_e, c, None) for c in range(3)] + [(full_h, c, courant) for c in range(3)]
    fields += [(full_t, c, courant * courant) for c in range(9)]
    top, bottom = slice(SUB - FULL, SUB), slice(SUB + rows, SUB + rows + FULL)
    for k, (full, c, factor) in enumerate(fields):
        packet = slice(k * FULL, (k + 1) * FULL)
        for at, get in ((top, low), (bottom, high)):
            value = get(packet)
            put(full, c, at, begin, value if factor is None else value * factor)
    base = len(fields) * FULL
    extra = [slice(base + i, base + i + 1) for i in range(EXTRA)]
    top, bottom = slice(SUB - HALO, SUB - FULL), slice(SUB + rows + FULL, SUB + rows + HALO)
    put(full_t, 0, top, begin, low(extra[0]) * (courant * courant))
    put(full_h, 1, top, begin, low(extra[1]) * courant)
    put(full_h, 2, top, begin, low(extra[2]) * courant)
    put(full_t, 1, bottom, begin, high(extra[0]) * (courant * courant))
    put(full_t, 2, bottom, begin, high(extra[1]) * (courant * courant))
    one = jnp.ones_like(low(extra[0]))
    put(full_e, 0, top, begin, one)
    put(full_e, 0, bottom, begin, one)


def sweeper(fe, fh, ft, fg, width):
    tiles = fe.shape[2] // SUB
    inside_x = jnp.where(lax.axis_index("gx") > 0, 1.0, 0.0).astype(jnp.float32)
    inside_y = jnp.where(lax.axis_index("gy") > 0, 1.0, 0.0).astype(jnp.float32)
    lane = lax.broadcasted_iota(jnp.int32, (SUB, LANE), 1)
    depths = [lax.rem(lane + n * LANE, NZ) for n in range(NZ // math.gcd(NZ, LANE))]
    uppers = [(d != NZ - 1).astype(jnp.float32) for d in depths]
    lowers = [(d != 0).astype(jnp.float32) for d in depths]

    sub = lax.broadcasted_iota(jnp.int32, (SUB, LANE), 0)
    joint = tiles - 1
    joint_mask = jnp.where(sub >= SUB // 2, inside_x, 1.0)

    def at(r, shift=0):
        return slice(r * SUB + shift, (r + 1) * SUB + shift)

    def tiles_of(before, after):
        return range((SIDE - before * NZ) // LANE, up_to(SIDE + width + after * NZ, LANE) // LANE)

    def ahead(values, places, n):
        turned = pltpu.roll(values[n], LANE - places, 1)
        if n + 1 not in values or (places == 1 and (n + 1) * LANE % NZ == 0):
            return turned
        return jnp.where(lane < LANE - places, turned, pltpu.roll(values[n + 1], LANE - places, 1))

    def behind(values, places, n):
        turned = pltpu.roll(values[n], places, 1)
        if n - 1 not in values or (places == 1 and n * LANE % NZ == 0):
            return turned
        return jnp.where(lane >= places, turned, pltpu.roll(values[n - 1], places, 1))

    def sweep(step, part):
        left = STEPS - 1 - step
        lanes_g, lanes_h, lanes_e = tiles_of(left + 1, left + 1), tiles_of(left + 1, left), tiles_of(left, left)
        last = left == 0
        g = [[{}, {}, {}] for _ in range(tiles)]
        h = [[{}, {}, {}] for _ in range(tiles)]
        joined = left + 1 <= SUB // 2
        if joined and left + 2 > SUB // 2:
            for full in (fe, fh, ft):
                for c in range(full.shape[0]):
                    for n in lanes_g:
                        full[c, n, at(joint), :] = jnp.where(
                            sub < SUB // 2, full[c, n, at(joint), :], full[c, n, at(0), :]
                        )

        def turn(r, n):
            e = [fe[c, n, at(r), :] for c in range(3)]
            for c in range(3):
                t = [ft[3 * i + c, n, at(r), :] for i in range(3)]
                g[r][c][n] = (t[0] * e[0] + t[1] * e[1]) + t[2] * e[2]
                if c > 0:
                    fg[c - 1, n, at(r), :] = g[r][c][n]
                    if joined and r == 1:
                        fg[c - 1, n, at(tiles), :] = g[r][c][n]

        def update_h(r, n):
            upper = uppers[n % len(uppers)]
            own = g[r]
            if r == tiles - 1 and not joined:
                next_x = [None] + [pltpu.roll(own[c][n], SUB - 1, 0) for c in (1, 2)]
            else:
                next_x = [None] + [fg[c - 1, n, at(r, 1), :] for c in (1, 2)]
            curl = [
                (ahead(own[2], NZ, n) - own[2][n]) - (ahead(own[1], 1, n) * upper - own[1][n]),
                (ahead(own[0], 1, n) * upper - own[0][n]) - (next_x[2] - own[2][n]),
                (next_x[1] - own[1][n]) - (ahead(own[0], NZ, n) - own[0][n]),
            ]
            for c in range(3):
                value = fh[c, n, at(r), :] - curl[c]
                if r == 0:
                    value = value * inside_x
                if r == joint and joined:
                    value = value * joint_mask
                if n < SIDE // LANE:
                    value = value * inside_y
                fh[c, n, at(r), :] = value
                if r == joint and joined and c > 0:
                    fh[c, n, at(0), :] = value
                h[r][c][n] = value

        def update_e(r, n):
            lower = lowers[n % len(lowers)]
            own = h[r]
            if r == 0:
                prev_x = [None] + [pltpu.roll(own[c][n], 1, 0) for c in (1, 2)]
            else:
                prev_x = [None] + [fh[c, n, at(r, -1), :] for c in (1, 2)]
            curl = [
                (own[2][n] - behind(own[2], NZ, n)) - (own[1][n] - behind(own[1], 1, n) * lower),
                (own[0][n] - behind(own[0], 1, n) * lower) - (own[2][n] - prev_x[2]),
                (own[1][n] - prev_x[1]) - (own[0][n] - behind(own[0], NZ, n)),
            ]
            for c in range(3):
                fe[c, n, at(r), :] = fe[c, n, at(r), :] + curl[c]

        inner = list(range(tiles - 2, 0, -1))
        if joined:
            stages = [(joint, None, None)] + [
                (r, r, r + 1 if n > 0 else None) for n, r in enumerate(inner)
            ]
            stages += [(None, joint, None), (None, None, 1)] + ([] if last else [(None, None, joint)])
        elif part == "inner":
            stages = [(inner[0], None, None)] + [
                (r, r, r + 1 if n > 0 else None) for n, r in enumerate(inner[1:])
            ]
        elif part == "rest":
            stages = [(joint, None, None), (joint - 1, joint, None), (None, joint - 1, joint), (1, None, joint - 1)]
            stages += [(0, None, None), (None, 0, 1), (None, None, 0)]
            h[1] = [{n: fh[c, n, at(1), :] for n in lanes_h} for c in range(3)]
        else:
            stages = [(r - 1, r, r + 1) for r in range(tiles, -2, -1)]
            stages = [[r if 0 <= r < tiles else None for r in stage] for stage in stages]
        for to_turn, to_h, to_e in stages:
            for n in lanes_g:
                if to_turn is not None:
                    turn(to_turn, n)
            for n in lanes_g:
                if to_h is not None and n in lanes_h:
                    update_h(to_h, n)
                if to_e is not None and n in lanes_e:
                    update_e(to_e, n)

    return sweep


def assemble_body(e_far, h_far, t_far, s_far, xa, xb, ya, yb, fe, fh, ft, saved, e_in, h_in, t_in, sems, fg):
    *copies, frames = fetch((e_far, h_far, t_far, s_far), (e_in, h_in, t_in, saved), sems)
    rows, width = e_in.shape[1:]
    total_rows = fe.shape[2]
    low_x, high_x = sorter("gx")
    low_y, high_y = sorter("gy")
    inner, top, bottom = slice(SUB, SUB + rows), slice(0, SUB), slice(SUB + rows, total_rows)
    fields = []
    for own, full, factor in ((e_in, fe, None), (h_in, fh, courant), (t_in, ft, courant * courant)):
        fields += [(own, full, factor, c) for c in range(own.shape[0])]
    count = len(fields)

    def scaled_to(factor, value):
        return value if factor is None else value * factor

    for k, (own, full, factor, c) in enumerate(fields):
        for n in range(full.shape[1]):
            full[c, n, top, :] = jnp.zeros((SUB, LANE), jnp.float32)
            full[c, n, bottom, :] = jnp.zeros((SUB, LANE), jnp.float32)
        for begin, side, tail in ((0, low_y, True), (SIDE + width, high_y, False)):
            value = side(from_lanes(ya, k, count, tail), from_lanes(yb, k, count, tail))
            put(full, c, inner, begin, scaled_to(factor, value))
    place_rows(fe, fh, ft, rows, SIDE, lambda s: low_x(xa[s], xb[s]), lambda s: high_x(xa[s], xb[s]))
    for copy in copies:
        copy.wait()
    for own, full, factor, c in fields:
        put(full, c, inner, SIDE, scaled_to(factor, own[c]))
    sweeper(fe, fh, ft, fg, width)(0, "inner")
    frames.wait()


def main_body(fe_in, fh_in, ft_in, saved, ca, cb, inverse, fe, fh, ft, scaled, to_a, to_b, fg):
    del fe_in, fh_in, ft_in
    rows, width = scaled.shape
    low_x, high_x = sorter("gx")
    low_y, high_y = sorter("gy")
    even_x = is_even("gx")

    height = up_to(FULL * 15 + EXTRA, 2 * SUB)
    for begin, side, tail in ((0, low_y, True), (SIDE + width, high_y, False)):
        packets = from_corners(side(ca[...], cb[...]), height, tail)
        low, high = low_x(*packets), high_x(*packets)
        place_rows(fe, fh, ft, rows, begin, lambda s, low=low: low[s], lambda s, high=high: high[s])

    sweep = sweeper(fe, fh, ft, fg, width)
    for step in range(STEPS):
        sweep(step, "rest" if step == 0 else "all")
        pair = 2 * SUB
        for r in range(rows // pair):
            for n in range(width // LANE):
                here = slice(r * pair, (r + 1) * pair)
                full = slice(SUB + r * pair, SUB + (r + 1) * pair)
                lanes = slice(n * LANE, (n + 1) * LANE)
                s = [saved[step, c, here, lanes].astype(jnp.float32) for c in range(3)]
                e = [fe[c, n + SIDE // LANE, full, :] for c in range(3)]
                term = (e[0] * s[0] + e[1] * s[1]) + e[2] * s[2]
                scaled[here, lanes] = term if step == 0 else scaled[here, lanes] + term

    scaled[...] = scaled[...] * inverse[...]
    head, tail = scaled[:RADIUS], scaled[rows - RADIUS :]
    to_a[...] = jnp.where(even_x, tail, head)
    to_b[...] = jnp.where(even_x, head, tail)


def emit_body(fe, fh, e_out, h_out):
    rows, width = e_out.shape[1:]
    for c in range(3):
        for n in range(width // LANE):
            lanes = slice(n * LANE, (n + 1) * LANE)
            e_out[c, :, lanes] = fe[c, n + SIDE // LANE, SUB : SUB + rows, :]
            h_out[c, :, lanes] = fh[c, n + SIDE // LANE, SUB : SUB + rows, :] * (1.0 / courant)


def box(values, unit, axis):
    size = values.shape[axis]

    def ahead(v, places):
        return pltpu.roll(v, size - places * unit, axis)

    two = values + ahead(values, 1)
    four = two + ahead(two, 2)
    eight = four + ahead(four, 4)
    return eight + ahead(values, 8)


def filter_rows(scaled, xa, xb, across, to_a, to_b):
    rows, width = scaled.shape
    even_y = is_even("gy")
    low, high = sorter("gx")
    a, b = xa[...], xb[...]
    extended = jnp.concatenate([low(a, b), scaled[...], high(a, b)], axis=0)
    result = box(box(extended, 1, 0), 1, 0)[:rows] * (1.0 / (RADIUS + 1.0))
    across[...] = result
    head, tail = result[:, :REACH], result[:, width - REACH :]
    to_a[...] = jnp.where(even_y, tail, head)
    to_b[...] = jnp.where(even_y, head, tail)


def filter_columns(across, ya, yb, gradient, made, sems):
    width = across.shape[1]
    low, high = sorter("gy")
    copies = []
    for r in range(across.shape[0] // SUB):
        at = slice(r * SUB, (r + 1) * SUB)
        a, b = ya[at], yb[at]
        extended = jnp.concatenate([low(a, b), across[at], high(a, b)], axis=1)
        made[at] = box(box(extended, NZ, 1), NZ, 1)[:, :width] * (1.0 / (RADIUS + 1.0))
        copies.append(pltpu.make_async_copy(made.at[at], gradient.at[at], sems.at[r]))
        copies[-1].start()
    for copy in copies:
        copy.wait()


def tent(offset):
    return (RADIUS + 1.0 - abs(offset)) / (RADIUS + 1.0)


def coverage(places, length):
    total = jnp.zeros(places.shape, jnp.float32)
    for offset in range(-RADIUS, RADIUS + 1):
        inside = ((places + offset >= 0) & (places + offset < length)).astype(jnp.float32)
        total = total + tent(offset) * inside
    return total


def shards(electric, magnetic, tensor, saved):
    rows, width = electric.shape[1:]
    cols = width // NZ
    edge = (RADIUS, width)
    full = ((width + 2 * SIDE) // LANE, rows + 2 * SUB, LANE)
    fulls = [(n, *full) for n in (3, 3, 9)]

    own = (electric, magnetic, tensor)
    xa, xb = swap(*pack_x(electric, magnetic, tensor), "gx", "gy")
    count = electric.shape[0] + magnetic.shape[0] + tensor.shape[0]
    packet = (count + -(-count // (2 * PER_TILE)), rows, WHOLE)
    ya, yb = swap(*call(pack_lanes, [packet, packet], own, room(*own), limit=8, far=(0, 1, 2)), "gy", "gx", fill=False)
    height = xa.shape[0]
    packet = (2 * height + up_to(height // 4, SUB), WHOLE)
    ca, cb = swap(*call(pack_corners, [packet, packet], (xa, xb), limit=8), "gy", "gx", apart=True)

    row_places = lax.axis_index("gx") * rows + lax.broadcasted_iota(jnp.int32, (rows, width), 0)
    col_places = lax.axis_index("gy") * cols + lax.broadcasted_iota(jnp.int32, (rows, width), 1) // NZ
    cover = coverage(row_places, lax.axis_size("gx") * rows) * coverage(col_places, lax.axis_size("gy") * cols)

    shifted = pltpu.VMEM((2, full[0], full[1] + SUB, LANE), jnp.float32)
    *fields, frames = call(
        assemble_body,
        [*fulls, jax.ShapeDtypeStruct(saved.shape, saved.dtype)],
        (*own, saved, xa, xb, ya, yb),
        [*room(*own)[:-1], pltpu.SemaphoreType.DMA((4,)), shifted],
        cost=2**22,
        far=(0, 1, 2, 3),
    )
    fe, fh, _, scaled, to_a, to_b = call(
        main_body,
        [*fulls, (rows, width), edge, edge],
        (*fields, frames, ca, cb, 1.0 / cover),
        [shifted],
        limit=20,
        aliases={0: 0, 1: 1, 2: 2},
        cost=2**23,
    )
    xa, xb = swap(to_a, to_b, "gx", "gy")
    e, h = call(emit_body, [electric.shape, magnetic.shape], (fe, fh))
    side = (rows, REACH)
    across, to_a, to_b = call(filter_rows, [(rows, width), side, side], (scaled, xa, xb))
    ya, yb = swap(to_a, to_b, "gy", "gx", apart=True)
    (gradient,) = call(
        filter_columns,
        [(rows, width)],
        (across, ya, yb),
        [pltpu.VMEM((rows, width), jnp.float32), pltpu.SemaphoreType.DMA((rows // SUB,))],
        space=pltpu.HBM,
    )
    return e, h, gradient


def solution(mesh):
    in_specs = (
        P(None, "gx", "gy"),
        P(None, "gx", "gy"),
        P(None, "gx", "gy"),
        P(None, None, "gx", "gy"),
    )
    out_specs = (P(None, "gx", "gy"), P(None, "gx", "gy"), P("gx", "gy"))
    return jax.shard_map(shards, mesh=mesh, in_specs=in_specs, out_specs=out_specs, check_vma=False)
```
